32 devices in a mesh: parts: 2 (over x), slab: 16 (over z, y, core).
Axes of the slice: x: 2, y: 2, z: 4, core: 2. Of those that a mesh axis runs over, the one named last changes fastest.
Arguments:
- volume: bfloat16 [32, 16, 64, 256], P(('parts', 'slab')), parts along dimension 0, may hold values from -6 to 6
- plane_weight: bfloat16 [2, 5, 5, 16, 256], replicated, may hold values from -0.3125 to 0.3125
- norm_gain: bfloat16 [2, 256], replicated, may hold values from 0.099609375 to 1.8984375
- expand_weight: bfloat16 [2, 256, 1024], replicated, may hold values from -0.375 to 0.375
- down_weight: bfloat16 [2, 1024, 256], replicated, may hold values from -0.1875 to 0.1875
- depth_weight: bfloat16 [2, 3, 256], replicated, may hold values from -3 to 3
Outputs:
- features: bfloat16 [32, 16, 64, 256], P(('parts', 'slab')), parts along dimension 0
The draws below stay inside these ranges and needn't reach their ends.
There are 2 independent parts, one for each index of `parts`. The reference program is written for one: setup_inputs(seed, part) draws one part's arguments, and reference() takes and returns one part's arrays. A program takes and returns all parts, laid end to end along the dimension named above; an argument that names none is the same for every part. Nothing has to cross between parts.
All inputs are finite; a program needn't handle non-finite values.
Results may differ from the reference program's by a relative error of at most 0.01.
Values may be sent and summed in bfloat16 or wider, within the bound.
No kernel may reach another device: no remote copies, remote signals or barrier semaphores. Data moves between devices by JAX's collectives and lax.ppermute only.
A program may use at most 64 MiB of HBM per device.

```python
import jax
import jax.numpy as jnp
from jax import lax

C = 256
HID = 1024
GROUP = 16
XW = 16
YW = 64
LAYERS = 2
FIRST_DILATION = 1
SECOND_DILATION = 4
Z = 16


def levels(key, dims, pieces, low, largest):
    level, own = 1.0, jax.random.fold_in(key, 6)
    for dim, parts in pieces:
        heights = jnp.exp(jax.random.uniform(jax.random.fold_in(own, dim), (parts,), jnp.float32, low / len(pieces), largest / len(pieces)))
        level = level * jnp.repeat(heights, dims[dim] // parts).reshape([-1 if axis == dim else 1 for axis in range(len(dims))])
    return level


def gaussian(key, extent, width, reach, cuts=(), held_as=jnp.bfloat16):
    loudness = levels(key, extent, cuts, -0.22, 0.18) if cuts else 1.0
    array = jax.random.normal(key, extent, jnp.float32) * width * loudness
    return jnp.minimum(jnp.maximum(array, -reach), reach).astype(held_as)


def setup_inputs(seed: int = 0, part: int = 0) -> dict:
    arg_keys = jax.random.split(jax.random.key(seed), 7)
    own_keys = jax.random.split(jax.random.fold_in(arg_keys[6], part), 7)
    volume = gaussian(own_keys[0], (Z, XW, YW, C), 1.0, 6.0, ((0, 16),))
    plane_weight = gaussian(arg_keys[1], (LAYERS, 5, 5, GROUP, C), (25 * GROUP) ** -0.5, 0.3125)
    norm_gain = jnp.clip(1.0 + 0.18 * jax.random.normal(arg_keys[2], (LAYERS, C), jnp.float32), 0.099609375, 1.8984375).astype(jnp.bfloat16)
    expand_weight = gaussian(arg_keys[3], (LAYERS, C, HID), C ** -0.5, 0.375)
    down_weight = gaussian(arg_keys[4], (LAYERS, HID, C), HID ** -0.5, 0.1875)
    depth_weight = gaussian(arg_keys[5], (LAYERS, 3, C), 0.6, 3.0)
    return dict(volume=volume, plane_weight=plane_weight, norm_gain=norm_gain, expand_weight=expand_weight, down_weight=down_weight, depth_weight=depth_weight)


epsilon = 1e-06

def plane_mix(plane_slice, weight, gain, up_matrix, down_matrix):
    extent_x, extent_y, channels = plane_slice.shape
    group_size = weight.shape[2]
    group_count = channels // group_size
    padded = jnp.pad(plane_slice.astype(jnp.float32), ((2, 2), (2, 2), (0, 0)))
    accumulated = jnp.zeros((extent_x, extent_y, group_count, group_size), jnp.float32)
    for offset_row in range(5):
        for offset_col in range(5):
            window = padded[offset_row:offset_row + extent_x, offset_col:offset_col + extent_y]
            window = window.reshape(extent_x, extent_y, group_count, group_size)
            kernel = weight[offset_row, offset_col].astype(jnp.float32).reshape(group_size, group_count, group_size)
            accumulated = accumulated + jnp.einsum('xyni,inj->xynj', window, kernel)
    conv_out = accumulated.reshape(extent_x, extent_y, channels)
    scale_inv = lax.rsqrt(lax.optimization_barrier(jnp.mean(conv_out * conv_out, axis=-1, keepdims=True)) + epsilon)
    normed = (conv_out * scale_inv * gain.astype(jnp.float32)).astype(jnp.bfloat16)
    hidden = jax.nn.silu(jnp.dot(normed.reshape(-1, channels), up_matrix, preferred_element_type=jnp.float32)).astype(jnp.bfloat16)
    mixed = jnp.dot(hidden, down_matrix, preferred_element_type=jnp.float32).astype(jnp.bfloat16)
    return mixed.reshape(extent_x, extent_y, channels)

def reference(volume, plane_weight, norm_gain, expand_weight, down_weight, depth_weight):
    current = volume
    for layer_number, dilation_factor in enumerate((FIRST_DILATION, SECOND_DILATION)):

        def slice_wise(plane_slice):
            return plane_mix(plane_slice, plane_weight[layer_number], norm_gain[layer_number], expand_weight[layer_number], down_weight[layer_number])
        mixed = lax.map(slice_wise, current)
        coeffs = depth_weight[layer_number].astype(jnp.float32)
        mixed_wide = mixed.astype(jnp.float32)
        total_slices = mixed.shape[0]
        padded = jnp.pad(mixed_wide, ((dilation_factor, dilation_factor), (0, 0), (0, 0), (0, 0)))
        depth_term = coeffs[0] * padded[:total_slices] + coeffs[1] * mixed_wide + coeffs[2] * padded[2 * dilation_factor:]
        depth_term = depth_term.astype(jnp.bfloat16)
        current = (current.astype(jnp.float32) + depth_term.astype(jnp.float32)).astype(jnp.bfloat16)
    return current
```

```python
import functools

import jax
import jax.numpy as jnp
from jax import lax
from jax.experimental import pallas as pl
from jax.experimental.pallas import tpu as pltpu
from jax.sharding import PartitionSpec as P

FIRST_DILATION = 1
SECOND_DILATION = 4
EPSILON = 1e-06
LANES = 128
PAIRS = 4

BF16 = jnp.bfloat16
F32 = jnp.float32


def exchanged(block, reach):
    size = lax.axis_size("slab")
    routes = ([], [])
    for i in range(size - reach):
        routes[i // reach % 2].extend([(i, i + reach), (i + reach, i)])
    return [lax.ppermute(block, "slab", route) for route in routes]


def ordered_coeffs(coeffs, reach):
    even = lax.rem(lax.div(lax.axis_index("slab"), reach), 2) == 0
    below, above = coeffs[0:1], coeffs[2:3]
    return jnp.where(even, above, below), coeffs[1:2], jnp.where(even, below, above)


def combined(base, own, first, second, coeffs):
    tap_first, tap_own, tap_second = coeffs
    term = tap_first * first.astype(F32) + tap_own * own.astype(F32) + tap_second * second.astype(F32)
    return (base.astype(F32) + term.astype(BF16).astype(F32)).astype(BF16)


def build_taps(taps, dense):
    group = taps.shape[2]
    lane_group = lax.broadcasted_iota(jnp.int32, (group, LANES), 1) // group

    def per_offset(dy, carry):
        for half in range(dense.shape[0]):
            lanes = slice(half * LANES, (half + 1) * LANES)
            for dx in range(5):
                tap = taps[dx, dy, :, lanes]
                for k in range(LANES // group):
                    value = jnp.where(lane_group == k, tap, jnp.zeros_like(tap))
                    for out in range(2):
                        row = (dx + out) * LANES + k * group
                        dense[half, dy, row : row + group, out * LANES : (out + 1) * LANES] = value
            for cell, out in ((5, 0), (0, 1)):
                rows = slice(cell * LANES, (cell + 1) * LANES)
                dense[half, dy, rows, out * LANES : (out + 1) * LANES] = jnp.zeros((LANES, LANES), BF16)
        return carry

    lax.fori_loop(0, 5, per_offset, 0)


def fill_shifts(row, x, shifted):
    count = row.shape[0]
    position = lax.broadcasted_iota(jnp.int32, row.shape, 0)
    for dy in range(5):
        step = dy - 2
        value = row
        if step:
            value = pltpu.roll(row, -step % count, 0)
            keep = position < count - step if step > 0 else position >= -step
            value = jnp.where(keep, value, 0.0)
        shifted[dy, x // 2 + 1, x % 2] = value.astype(BF16)


def conv_normed(first_pair, shifted, dense, gain, normed):
    count, width = shifted.shape[3], shifted.shape[4]
    sums = []
    for half in range(width // LANES):
        lanes = slice(half * LANES, (half + 1) * LANES)
        total = None
        for dy in range(5):
            pieces = [
                shifted[dy, pl.ds(first_pair + block, PAIRS), i, :, lanes].reshape(PAIRS * count, LANES)
                for block in range(3)
                for i in range(2)
            ]
            part = jnp.dot(jnp.concatenate(pieces, axis=-1), dense[half, dy], preferred_element_type=F32)
            total = part if total is None else total + part
        sums.append(total)
    for out in range(2):
        parts = [total[:, out * LANES : (out + 1) * LANES] for total in sums]
        squares = sum(part * part for part in parts)
        scale = lax.rsqrt(jnp.sum(squares, axis=-1, keepdims=True) / width + EPSILON)
        value = jnp.concatenate([part * scale for part in parts], axis=-1) * gain
        normed[:, out] = value.astype(BF16).reshape(PAIRS, count, width)


def silu(value):
    half = 0.5 * value
    return half + half * jnp.tanh(half)


def mlp(rows, up, down, hidden):
    for start in range(0, up.shape[1], 256):
        value = jnp.dot(rows, up[:, start : start + 256], preferred_element_type=F32)
        hidden[:, start : start + 256] = silu(value).astype(BF16)
    return jnp.dot(hidden[...], down[...], preferred_element_type=F32).astype(BF16)


def block_kernel(layer, reach, *refs):
    if reach is None:
        taps_hbm, up_hbm, down_hbm, gain_ref, base, mixed = refs[:6]
    else:
        taps_hbm, up_hbm, down_hbm, gain_ref, coeff_ref, base, own, first, second, current, mixed = refs[:11]
    taps, up, down, dense, shifted, normed, hidden, sems = refs[-8:]
    copies = [
        pltpu.make_async_copy(source.at[layer], target, sems.at[k])
        for k, (source, target) in enumerate(((taps_hbm, taps), (up_hbm, up), (down_hbm, down)))
    ]
    for copy in copies:
        copy.start()
    extent_x, extent_y, channels = base.shape
    for x in (-2, -1, extent_x, extent_x + 1):
        shifted[:, x // 2 + 1, x % 2] = jnp.zeros((5, extent_y, channels), BF16)
    if reach is not None:
        coeffs = ordered_coeffs(coeff_ref[layer - 1].astype(F32), reach)
    for x in range(extent_x):
        row = base[x]
        if reach is not None:
            row = combined(row, own[x], first[x], second[x], coeffs)
            current[x] = row
        fill_shifts(row.astype(F32), x, shifted)
    copies[0].wait()
    build_taps(taps, dense)
    copies[1].wait()
    copies[2].wait()
    gain = gain_ref[layer : layer + 1].astype(F32)
    chunks = extent_x // (2 * PAIRS)
    for chunk in range(chunks + 1):
        if chunk < chunks:
            conv_normed(chunk * PAIRS, shifted, dense, gain, normed.at[chunk % 2])
        if chunk > 0:
            slot = (chunk - 1) % 2
            rows = normed[slot].reshape(PAIRS * 2 * extent_y, channels)
            result = mlp(rows, up, down, hidden.at[slot])
            mixed[pl.ds((chunk - 1) * PAIRS * 2, PAIRS * 2)] = result.reshape(PAIRS * 2, extent_y, channels)


def block(layer, reach, taps, up, down, gain, coeffs, *arrays):
    extent_x, extent_y, channels = arrays[0].shape
    wide = up.shape[2]
    anywhere, vmem = pl.BlockSpec(memory_space=pltpu.HBM), pl.BlockSpec(memory_space=pltpu.VMEM)
    shape = jax.ShapeDtypeStruct((extent_x, extent_y, channels), BF16)
    small = (gain,) if reach is None else (gain, coeffs)
    outputs = 1 if reach is None else 2
    rows = PAIRS * 2 * extent_y
    return pl.pallas_call(
        functools.partial(block_kernel, layer, reach),
        out_shape=[shape] * outputs,
        in_specs=[anywhere] * 3 + [vmem] * (len(small) + len(arrays)),
        out_specs=[vmem] * outputs,
        scratch_shapes=[
            pltpu.VMEM(taps.shape[1:], BF16),
            pltpu.VMEM(up.shape[1:], BF16),
            pltpu.VMEM(down.shape[1:], BF16),
            pltpu.VMEM((channels // LANES, 5, 6 * LANES, 2 * LANES), BF16),
            pltpu.VMEM((5, extent_x // 2 + 2, 2, extent_y, channels), BF16),
            pltpu.VMEM((2, PAIRS, 2, extent_y, channels), BF16),
            pltpu.VMEM((2, rows, wide), BF16),
            pltpu.SemaphoreType.DMA((3,)),
        ],
        compiler_params=pltpu.CompilerParams(vmem_limit_bytes=32 << 20),
        name=f"block{layer}",
    )(taps, up, down, *small, *arrays)


def final_kernel(layer, reach, coeff_ref, base, own, first, second, out):
    coeffs = ordered_coeffs(coeff_ref[layer].astype(F32), reach)
    for x in range(base.shape[0]):
        out[x] = combined(base[x], own[x], first[x], second[x], coeffs)


def final(layer, reach, coeffs, *arrays):
    vmem = pl.BlockSpec(memory_space=pltpu.VMEM)
    return pl.pallas_call(
        functools.partial(final_kernel, layer, reach),
        out_shape=jax.ShapeDtypeStruct(arrays[0].shape, BF16),
        in_specs=[vmem] * 5,
        out_specs=vmem,
        compiler_params=pltpu.CompilerParams(vmem_limit_bytes=8 << 20),
        name="final",
    )(coeffs, *arrays)


def shards(volume, plane_weight, norm_gain, expand_weight, down_weight, depth_weight):
    depth = volume.shape[0]
    reaches = (FIRST_DILATION // depth, SECOND_DILATION // depth)
    weights = (plane_weight, expand_weight, down_weight, norm_gain, depth_weight)
    (mixed,) = block(0, None, *weights, volume[0])
    current, mixed2 = block(1, reaches[0], *weights, volume[0], mixed, *exchanged(mixed, reaches[0]))
    return final(1, reaches[1], depth_weight, current, mixed2, *exchanged(mixed2, reaches[1]))[None]


def solution(mesh):
    placed = (P(("parts", "slab"), None, None, None), P(), P(), P(), P(), P())
    return jax.shard_map(
        shards,
        mesh=mesh,
        in_specs=placed,
        out_specs=P(("parts", "slab"), None, None, None),
        check_vma=False,
    )
```

```python
import functools

import jax
import jax.numpy as jnp
from jax import lax
from jax.experimental import pallas as pl
from jax.experimental.pallas import tpu as pltpu
from jax.sharding import PartitionSpec as P

FIRST_DILATION = 1
SECOND_DILATION = 4
EPSILON = 1e-06
LANES = 128
MARGIN = 2
TILE_FLOPS = 2 * 64 * 256 * (3840 + 2 * 1024)

BF16 = jnp.bfloat16
F32 = jnp.float32
VMEM = pl.BlockSpec(memory_space=pltpu.VMEM)
HBM = pl.BlockSpec(memory_space=pltpu.HBM)


def exchanged(block, reach):
    size = lax.axis_size("slab")
    routes = ([], [])
    for i in range(size - reach):
        routes[i // reach % 2].extend([(i, i + reach), (i + reach, i)])
    return [lax.ppermute(block, "slab", route) for route in routes]


def ordered_coeffs(coeffs, reach):
    even = lax.rem(lax.div(lax.axis_index("slab"), reach), 2) == 0
    below, above = coeffs[0:1], coeffs[2:3]
    return jnp.where(even, above, below), coeffs[1:2], jnp.where(even, below, above)


def combined(base, own, first, second, coeffs):
    tap_first, tap_own, tap_second = coeffs
    term = tap_first * first.astype(F32) + tap_own * own.astype(F32) + tap_second * second.astype(F32)
    return (base.astype(F32) + term.astype(BF16).astype(F32)).astype(BF16)


def build_taps(taps, dense):
    group = taps.shape[2]
    lane_group = lax.broadcasted_iota(jnp.int32, (group, LANES), 1) // group

    for dy in range(5):
        for half in range(dense.shape[0]):
            lanes = slice(half * LANES, (half + 1) * LANES)
            for dx in range(5):
                tap = taps[dx, dy, :, lanes]
                for k in range(LANES // group):
                    value = jnp.where(lane_group == k, tap, jnp.zeros_like(tap))
                    for out in range(2):
                        row = (dx + out) * LANES + k * group
                        dense[half, dy, row : row + group, out * LANES : (out + 1) * LANES] = value
            for cell, out in ((5, 0), (0, 1)):
                rows = slice(cell * LANES, (cell + 1) * LANES)
                dense[half, dy, rows, out * LANES : (out + 1) * LANES] = jnp.zeros((LANES, LANES), BF16)


def fill_shifts(row, x, shifted):
    count = row.shape[0]
    position = lax.broadcasted_iota(jnp.int32, row.shape, 0)
    for dy in range(5):
        step = dy - 2
        value = row
        if step:
            value = pltpu.roll(row, -step % count, 0)
            keep = position < count - step if step > 0 else position >= -step
            value = jnp.where(keep, value, 0.0)
        shifted[dy, x // 2, x % 2] = value.astype(BF16)


def clear_row(x, shifted):
    shifted[:, x // 2, x % 2] = jnp.zeros((5,) + shifted.shape[3:], BF16)


def conv_normed(first_pair, pairs, shifted, dense, gain, normed):
    count, width = shifted.shape[3], shifted.shape[4]
    sums = []
    for half in range(width // LANES):
        lanes = slice(half * LANES, (half + 1) * LANES)
        total = None
        for dy in range(5):
            pieces = [
                shifted[dy, first_pair + block : first_pair + block + pairs, i, :, lanes].reshape(pairs * count, LANES)
                for block in range(3)
                for i in range(2)
            ]
            part = jnp.dot(jnp.concatenate(pieces, axis=-1), dense[half, dy], preferred_element_type=F32)
            total = part if total is None else total + part
        sums.append(total)
    for out in range(2):
        parts = [total[:, out * LANES : (out + 1) * LANES] for total in sums]
        squares = sum(part * part for part in parts)
        scale = lax.rsqrt(jnp.sum(squares, axis=-1, keepdims=True) / width + EPSILON)
        value = jnp.concatenate([part * scale for part in parts], axis=-1) * gain
        normed[:pairs, out] = value.astype(BF16).reshape(pairs, count, width)


def silu(value):
    half = 0.5 * value
    return half + half * jnp.tanh(half)


def mlp(rows, up, down, hidden):
    for start in range(0, up.shape[1], 256):
        value = jnp.dot(rows, up[:, start : start + 256], preferred_element_type=F32)
        hidden[:, start : start + 256] = silu(value).astype(BF16)
    return jnp.dot(hidden[...], down[...], preferred_element_type=F32).astype(BF16)


def mix(chunks, shifted, dense, gain, up, down, normed, hidden, mixed, copies=()):
    count, channels = shifted.shape[3:]
    starts = [sum(chunks[:k]) for k in range(len(chunks))]
    for k in range(len(chunks) + 1):
        if k < len(chunks):
            conv_normed(starts[k], chunks[k], shifted, dense, gain, normed.at[k % 2])
        if k == 1:
            for copy in copies:
                copy.wait()
        if k > 0:
            pairs, first = chunks[k - 1], starts[k - 1]
            rows = normed[(k - 1) % 2, :pairs].reshape(pairs * 2 * count, channels)
            result = mlp(rows, up, down, hidden.at[(k - 1) % 2, : pairs * 2 * count])
            mixed[first * 2 : (first + pairs) * 2] = result.reshape(pairs * 2, count, channels)


def call(body, name, outputs, inputs, in_specs, scratch, pairs=0):
    return pl.pallas_call(
        body,
        out_shape=outputs,
        in_specs=in_specs,
        out_specs=[VMEM] * len(outputs),
        scratch_shapes=scratch,
        compiler_params=pltpu.CompilerParams(vmem_limit_bytes=24 << 20),
        cost_estimate=pl.CostEstimate(flops=max(1, pairs) * 4 * TILE_FLOPS, bytes_accessed=1 << 20, transcendentals=0),
        name=name,
    )(*inputs)


def split(pairs):
    return (pairs,)


def mix_scratch(chunks, count, channels, wide):
    most = max(chunks)
    return [
        pltpu.VMEM((5, sum(chunks) + 2, 2, count, channels), BF16),
        pltpu.VMEM((2, most, 2, count, channels), BF16),
        pltpu.VMEM((2, most * 2 * count, wide), BF16),
    ]


def in_hbm(array):
    return pltpu.with_memory_space_constraint(array, pltpu.HBM)


def copies_in(pairs, sems):
    copies = [pltpu.make_async_copy(source, target, sems.at[k]) for k, (source, target) in enumerate(pairs)]
    for copy in copies:
        copy.start()
    return copies


def first_a_kernel(chunks, volume, taps_hbm, up_hbm, down_hbm, gain_hbm, mixed, rows, taps, up, down, gain, dense, shifted, normed, hidden, sems):
    front = shifted.shape[1] * 2 - MARGIN
    copies = copies_in(
        (
            (taps_hbm.at[0], taps.at[0]),
            (volume.at[0, :front], rows.at[:front]),
            (gain_hbm, gain),
            (up_hbm.at[0], up),
            (down_hbm.at[0], down),
            (volume.at[0, front:], rows.at[front:]),
            (taps_hbm.at[1], taps.at[1]),
        ),
        sems,
    )
    clear_row(0, shifted)
    clear_row(1, shifted)
    copies[0].wait()
    build_taps(taps.at[0], dense)
    copies[1].wait()
    for x in range(front):
        fill_shifts(rows[x].astype(F32), x + MARGIN, shifted)
    copies[2].wait()
    mix(chunks, shifted, dense, gain[0:1].astype(F32), up, down, normed, hidden, mixed, copies[3:5])
    copies[5].wait()
    copies[6].wait()


def first_b_kernel(chunks, rows, taps, up, down, gain, dense, up_hbm, down_hbm, mixed, up_next, down_next, dense_next, shifted, normed, hidden, sems):
    copies = copies_in(((up_hbm.at[1], up_next), (down_hbm.at[1], down_next)), sems)
    filled = shifted.shape[1] * 2 - MARGIN
    clear_row(filled, shifted)
    clear_row(filled + 1, shifted)
    for x in range(filled):
        fill_shifts(rows[rows.shape[0] - filled + x].astype(F32), x, shifted)
    mix(chunks, shifted, dense, gain[0:1].astype(F32), up, down, normed, hidden, mixed)
    build_taps(taps.at[1], dense_next)
    for copy in copies:
        copy.wait()


def second_a_kernel(chunks, reach, rows, own, first, second, up, down, gain, dense, coeffs, current, mixed, shifted, normed, hidden):
    clear_row(0, shifted)
    clear_row(1, shifted)
    taps = ordered_coeffs(coeffs[0].astype(F32), reach)
    for x in range(own.shape[0]):
        row = combined(rows[x], own[x], first[x], second[x], taps)
        current[x] = row
        fill_shifts(row.astype(F32), x + MARGIN, shifted)
    mix(chunks, shifted, dense, gain[1:2].astype(F32), up, down, normed, hidden, mixed)


def second_b_kernel(chunks, reach, rows, current_a, own, first, second, up, down, gain, dense, coeffs, current, mixed, shifted, normed, hidden):
    filled = shifted.shape[1] * 2
    clear_row(filled - 2, shifted)
    clear_row(filled - 1, shifted)
    before = filled - MARGIN - own.shape[0]
    for x in range(before):
        fill_shifts(current_a[current_a.shape[0] - before + x].astype(F32), x, shifted)
    taps = ordered_coeffs(coeffs[0].astype(F32), reach)
    for x in range(own.shape[0]):
        row = combined(rows[current_a.shape[0] + x], own[x], first[x], second[x], taps)
        current[x] = row
        fill_shifts(row.astype(F32), before + x, shifted)
    mix(chunks, shifted, dense, gain[1:2].astype(F32), up, down, normed, hidden, mixed)


def final_a_kernel(reach, coeff_ref, current, own, first, second, out, rows, sem):
    finish(reach, coeff_ref, [current[x] for x in range(rows.shape[0])], own, first, second, out, rows, sem, 0)


def final_b_kernel(reach, coeff_ref, current_a, current_b, own, first, second, before, out, rows, sem):
    kept = current_a.shape[0] + current_b.shape[0] - rows.shape[0]
    bases = [current_a[x] for x in range(kept, current_a.shape[0])] + [current_b[x] for x in range(current_b.shape[0])]
    finish(reach, coeff_ref, bases, own, first, second, out, rows, sem, kept)


def finish(reach, coeff_ref, bases, own, first, second, out, rows, sem, start):
    coeffs = ordered_coeffs(coeff_ref[1].astype(F32), reach)
    for x, base in enumerate(bases):
        rows[x] = combined(base, own[x], first[x], second[x], coeffs)
    copy = pltpu.make_async_copy(rows, out.at[0, start : start + rows.shape[0]], sem)
    copy.start()
    copy.wait()


def final(body, name, shape, rows, aliases, *inputs):
    return pl.pallas_call(
        body,
        out_shape=pltpu.HBM(shape, BF16),
        in_specs=[VMEM] * (len(inputs) - len(aliases)) + [HBM] * len(aliases),
        out_specs=HBM,
        scratch_shapes=[pltpu.VMEM((rows,) + shape[2:], BF16), pltpu.SemaphoreType.DMA],
        input_output_aliases=aliases,
        compiler_params=pltpu.CompilerParams(vmem_limit_bytes=8 << 20),
        cost_estimate=pl.CostEstimate(flops=1 << 20, bytes_accessed=1 << 20, transcendentals=0),
        name=name,
    )(*inputs)


def shards(volume, plane_weight, norm_gain, expand_weight, down_weight, depth_weight):
    depth, extent, count, channels = volume.shape
    wide = expand_weight.shape[2]
    reaches = (FIRST_DILATION // depth, SECOND_DILATION // depth)
    volume, plane_weight, norm_gain, expand_weight, down_weight = map(
        in_hbm, (volume, plane_weight, norm_gain, expand_weight, down_weight)
    )

    def array(*shape):
        return jax.ShapeDtypeStruct(shape, BF16)

    def plane(rows):
        return array(rows, count, channels)

    dense_shape = array(channels // LANES, 5, 6 * LANES, 2 * LANES)
    up_shape, down_shape = array(*expand_weight.shape[1:]), array(*down_weight.shape[1:])
    half = extent // 2
    front, back = half + MARGIN, half - MARGIN

    def scratch(chunks, copies=0):
        return mix_scratch(chunks, count, channels, wide) + [pltpu.SemaphoreType.DMA((copies,))] * (copies > 0)

    chunks = split(front // 2)
    mixed_a, rows, taps, up, down, gain, dense = call(
        functools.partial(first_a_kernel, chunks), "first_a",
        [plane(front), plane(extent), array(*plane_weight.shape), up_shape, down_shape, array(*norm_gain.shape), dense_shape],
        (volume, plane_weight, expand_weight, down_weight, norm_gain), [HBM] * 5, scratch(chunks, 7), front // 2,
    )
    got_a = exchanged(mixed_a, reaches[0])
    chunks = split(back // 2)
    mixed_b, up_next, down_next, dense_next = call(
        functools.partial(first_b_kernel, chunks), "first_b", [plane(back), up_shape, down_shape, dense_shape],
        (rows, taps, up, down, gain, dense, expand_weight, down_weight), [VMEM] * 6 + [HBM] * 2,
        scratch(chunks, 2), back // 2,
    )
    got_b = exchanged(mixed_b, reaches[0])
    shared = (up_next, down_next, gain, dense_next, depth_weight)
    chunks = split(half // 2)
    current_a, wide_a = call(
        functools.partial(second_a_kernel, chunks, reaches[0]), "second_a", [plane(front), plane(half)],
        (rows, mixed_a, *got_a, *shared), [VMEM] * 9, scratch(chunks), half // 2,
    )
    far_a = exchanged(wide_a, reaches[1])
    current_b, wide_b = call(
        functools.partial(second_b_kernel, chunks, reaches[0]), "second_b", [plane(back), plane(half)],
        (rows, current_a, mixed_b, *got_b, *shared), [VMEM] * 10, scratch(chunks), half // 2,
    )
    far_b = exchanged(wide_b, reaches[1])
    features = final(
        functools.partial(final_a_kernel, reaches[1]), "final_a", volume.shape, half, {},
        depth_weight, current_a, wide_a, *far_a,
    )
    return final(
        functools.partial(final_b_kernel, reaches[1]), "final_b", volume.shape, half, {6: 0},
        depth_weight, current_a, current_b, wide_b, *far_b, features,
    )


def solution(mesh):
    placed = (P(("parts", "slab"), None, None, None), P(), P(), P(), P(), P())
    return jax.shard_map(
        shards,
        mesh=mesh,
        in_specs=placed,
        out_specs=P(("parts", "slab"), None, None, None),
        check_vma=False,
    )
```

```python
import functools

import jax
import jax.numpy as jnp
from jax import lax
from jax.experimental import pallas as pl
from jax.experimental.pallas import tpu as pltpu
from jax.sharding import PartitionSpec as P

FIRST_DILATION = 1
SECOND_DILATION = 4
EPSILON = 1e-06
LANES = 128
MARGIN = 2
TILE_FLOPS = 2 * 64 * 256 * (3840 + 2 * 1024)

BF16 = jnp.bfloat16
F32 = jnp.float32
VMEM = pl.BlockSpec(memory_space=pltpu.VMEM)
HBM = pl.BlockSpec(memory_space=pltpu.HBM)


def swapped(block, pairs):
    parts, size = lax.axis_size("parts"), lax.axis_size("slab")
    partner = {}
    for a, b in pairs:
        partner[a], partner[b] = b, a
    routes = []
    for part in range(parts):
        for i in range(size):
            if i in partner:
                routes.append((part * size + i, part * size + partner[i]))
            elif (part ^ 1) < parts:
                routes.append((part * size + i, (part ^ 1) * size + i))
    return lax.ppermute(block, ("parts", "slab"), routes)


def exchanged(block, reach):
    size = lax.axis_size("slab")
    return [swapped(block, [(i, i + reach) for i in range(size - reach) if i // reach % 2 == odd]) for odd in range(2)]


def ordered_coeffs(coeffs, reach):
    place = lax.axis_index("slab")
    even = lax.rem(lax.div(place, reach), 2) == 0
    below = jnp.where(place >= reach, coeffs[0:1], 0.0)
    above = jnp.where(place + reach < lax.axis_size("slab"), coeffs[2:3], 0.0)
    return jnp.where(even, above, below), coeffs[1:2], jnp.where(even, below, above)


def combined(base, own, first, second, coeffs):
    tap_first, tap_own, tap_second = coeffs
    term = tap_first * first.astype(F32) + tap_own * own.astype(F32) + tap_second * second.astype(F32)
    return (base.astype(F32) + term.astype(BF16).astype(F32)).astype(BF16)


def build_taps(taps, dense):
    group = taps.shape[2]
    lane_group = lax.broadcasted_iota(jnp.int32, (group, LANES), 1) // group

    for dy in range(5):
        for half in range(dense.shape[0]):
            lanes = slice(half * LANES, (half + 1) * LANES)
            for dx in range(5):
                tap = taps[dx, dy, :, lanes]
                for k in range(LANES // group):
                    value = jnp.where(lane_group == k, tap, jnp.zeros_like(tap))
                    for out in range(2):
                        row = (dx + out) * LANES + k * group
                        dense[half, dy, row : row + group, out * LANES : (out + 1) * LANES] = value
            for cell, out in ((5, 0), (0, 1)):
                rows = slice(cell * LANES, (cell + 1) * LANES)
                dense[half, dy, rows, out * LANES : (out + 1) * LANES] = jnp.zeros((LANES, LANES), BF16)


def fill_shifts(row, x, shifted):
    count = row.shape[0]
    position = lax.broadcasted_iota(jnp.int32, row.shape, 0)
    for dy in range(5):
        step = dy - 2
        value = row
        if step:
            value = pltpu.roll(row, -step % count, 0)
            keep = position < count - step if step > 0 else position >= -step
            value = jnp.where(keep, value, 0.0)
        shifted[dy, x // 2, x % 2] = value.astype(BF16)


def clear_row(x, shifted):
    shifted[:, x // 2, x % 2] = jnp.zeros((5,) + shifted.shape[3:], BF16)


def conv_normed(first_pair, pairs, shifted, dense, gain, normed):
    count, width = shifted.shape[3], shifted.shape[4]
    sums = []
    for half in range(width // LANES):
        lanes = slice(half * LANES, (half + 1) * LANES)
        total = None
        for dy in range(5):
            pieces = [
                shifted[dy, first_pair + block : first_pair + block + pairs, i, :, lanes].reshape(pairs * count, LANES)
                for block in range(3)
                for i in range(2)
            ]
            part = jnp.dot(jnp.concatenate(pieces, axis=-1), dense[half, dy], preferred_element_type=F32)
            total = part if total is None else total + part
        sums.append(total)
    for out in range(2):
        parts = [total[:, out * LANES : (out + 1) * LANES] for total in sums]
        squares = sum(part * part for part in parts)
        scale = lax.rsqrt(jnp.sum(squares, axis=-1, keepdims=True) / width + EPSILON)
        value = jnp.concatenate([part * scale for part in parts], axis=-1) * gain
        normed[:pairs, out] = value.astype(BF16).reshape(pairs, count, width)


def silu(value):
    half = 0.5 * value
    return half + half * jnp.tanh(half)


def mlp(rows, up, down, hidden):
    for start in range(0, up.shape[1], 256):
        value = jnp.dot(rows, up[:, start : start + 256], preferred_element_type=F32)
        hidden[:, start : start + 256] = silu(value).astype(BF16)
    return jnp.dot(hidden[...], down[...], preferred_element_type=F32).astype(BF16)


def mix(chunks, shifted, dense, gain, up, down, normed, hidden, mixed, copies=()):
    count, channels = shifted.shape[3:]
    starts = [sum(chunks[:k]) for k in range(len(chunks))]
    for k in range(len(chunks) + 1):
        if k < len(chunks):
            conv_normed(starts[k], chunks[k], shifted, dense, gain, normed.at[k % 2])
        if k == 1:
            for copy in copies:
                copy.wait()
        if k > 0:
            pairs, first = chunks[k - 1], starts[k - 1]
            rows = normed[(k - 1) % 2, :pairs].reshape(pairs * 2 * count, channels)
            result = mlp(rows, up, down, hidden.at[(k - 1) % 2, : pairs * 2 * count])
            mixed[first * 2 : (first + pairs) * 2] = result.reshape(pairs * 2, count, channels)


def call(body, name, outputs, inputs, in_specs, scratch, pairs=0):
    return pl.pallas_call(
        body,
        out_shape=outputs,
        in_specs=in_specs,
        out_specs=[VMEM] * len(outputs),
        scratch_shapes=scratch,
        compiler_params=pltpu.CompilerParams(vmem_limit_bytes=24 << 20),
        cost_estimate=pl.CostEstimate(flops=max(1, pairs) * 4 * TILE_FLOPS, bytes_accessed=1 << 20, transcendentals=0),
        name=name,
    )(*inputs)


def split(pairs):
    return (pairs,)


def mix_scratch(chunks, count, channels, wide):
    most = max(chunks)
    return [
        pltpu.VMEM((5, sum(chunks) + 2, 2, count, channels), BF16),
        pltpu.VMEM((2, most, 2, count, channels), BF16),
        pltpu.VMEM((2, most * 2 * count, wide), BF16),
    ]


def in_hbm(array):
    return pltpu.with_memory_space_constraint(array, pltpu.HBM)


def copies_in(pairs, sems):
    copies = [pltpu.make_async_copy(source, target, sems.at[k]) for k, (source, target) in enumerate(pairs)]
    for copy in copies:
        copy.start()
    return copies


def first_a_kernel(chunks, volume, taps_hbm, up_hbm, down_hbm, gain_hbm, mixed, rows, taps, up, down, gain, dense, shifted, normed, hidden, sems):
    front = shifted.shape[1] * 2 - MARGIN
    copies = copies_in(
        (
            (taps_hbm.at[0], taps.at[0]),
            (volume.at[0, :front], rows.at[:front]),
            (gain_hbm, gain),
            (up_hbm.at[0], up),
            (down_hbm.at[0], down),
            (volume.at[0, front:], rows.at[front:]),
            (taps_hbm.at[1], taps.at[1]),
        ),
        sems,
    )
    clear_row(0, shifted)
    clear_row(1, shifted)
    copies[0].wait()
    build_taps(taps.at[0], dense)
    copies[1].wait()
    for x in range(front):
        fill_shifts(rows[x].astype(F32), x + MARGIN, shifted)
    copies[2].wait()
    mix(chunks, shifted, dense, gain[0:1].astype(F32), up, down, normed, hidden, mixed, copies[3:5])
    copies[5].wait()
    copies[6].wait()


def first_b_kernel(chunks, rows, taps, up, down, gain, dense, up_hbm, down_hbm, mixed, up_next, down_next, dense_next, shifted, normed, hidden, sems):
    copies = copies_in(((up_hbm.at[1], up_next), (down_hbm.at[1], down_next)), sems)
    filled = shifted.shape[1] * 2 - MARGIN
    clear_row(filled, shifted)
    clear_row(filled + 1, shifted)
    for x in range(filled):
        fill_shifts(rows[rows.shape[0] - filled + x].astype(F32), x, shifted)
    mix(chunks, shifted, dense, gain[0:1].astype(F32), up, down, normed, hidden, mixed)
    build_taps(taps.at[1], dense_next)
    for copy in copies:
        copy.wait()


def second_a_kernel(chunks, reach, rows, own, first, second, up, down, gain, dense, coeffs, current, mixed, shifted, normed, hidden):
    clear_row(0, shifted)
    clear_row(1, shifted)
    taps = ordered_coeffs(coeffs[0].astype(F32), reach)
    for x in range(own.shape[0]):
        row = combined(rows[x], own[x], first[x], second[x], taps)
        current[x] = row
        fill_shifts(row.astype(F32), x + MARGIN, shifted)
    mix(chunks, shifted, dense, gain[1:2].astype(F32), up, down, normed, hidden, mixed)


def second_b_kernel(chunks, reach, rows, current_a, own, first, second, up, down, gain, dense, coeffs, current, mixed, shifted, normed, hidden):
    filled = shifted.shape[1] * 2
    clear_row(filled - 2, shifted)
    clear_row(filled - 1, shifted)
    before = filled - MARGIN - own.shape[0]
    for x in range(before):
        fill_shifts(current_a[current_a.shape[0] - before + x].astype(F32), x, shifted)
    taps = ordered_coeffs(coeffs[0].astype(F32), reach)
    for x in range(own.shape[0]):
        row = combined(rows[current_a.shape[0] + x], own[x], first[x], second[x], taps)
        current[x] = row
        fill_shifts(row.astype(F32), before + x, shifted)
    mix(chunks, shifted, dense, gain[1:2].astype(F32), up, down, normed, hidden, mixed)


def final_a_kernel(reach, coeff_ref, current, own, first, second, out, rows, sem):
    finish(reach, coeff_ref, [current[x] for x in range(rows.shape[0])], own, first, second, out, rows, sem, 0)


def final_b_kernel(reach, coeff_ref, current_a, current_b, own, first, second, before, out, rows, sem):
    kept = current_a.shape[0] + current_b.shape[0] - rows.shape[0]
    bases = [current_a[x] for x in range(kept, current_a.shape[0])] + [current_b[x] for x in range(current_b.shape[0])]
    finish(reach, coeff_ref, bases, own, first, second, out, rows, sem, kept)


def finish(reach, coeff_ref, bases, own, first, second, out, rows, sem, start):
    coeffs = ordered_coeffs(coeff_ref[1].astype(F32), reach)
    for x, base in enumerate(bases):
        rows[x] = combined(base, own[x], first[x], second[x], coeffs)
    copy = pltpu.make_async_copy(rows, out.at[0, start : start + rows.shape[0]], sem)
    copy.start()
    copy.wait()


def final(body, name, shape, rows, aliases, *inputs):
    return pl.pallas_call(
        body,
        out_shape=pltpu.HBM(shape, BF16),
        in_specs=[VMEM] * (len(inputs) - len(aliases)) + [HBM] * len(aliases),
        out_specs=HBM,
        scratch_shapes=[pltpu.VMEM((rows,) + shape[2:], BF16), pltpu.SemaphoreType.DMA],
        input_output_aliases=aliases,
        compiler_params=pltpu.CompilerParams(vmem_limit_bytes=8 << 20),
        cost_estimate=pl.CostEstimate(flops=1 << 20, bytes_accessed=1 << 20, transcendentals=0),
        name=name,
    )(*inputs)


def shards(volume, plane_weight, norm_gain, expand_weight, down_weight, depth_weight):
    depth, extent, count, channels = volume.shape
    wide = expand_weight.shape[2]
    reaches = (FIRST_DILATION // depth, SECOND_DILATION // depth)
    volume, plane_weight, norm_gain, expand_weight, down_weight = map(
        in_hbm, (volume, plane_weight, norm_gain, expand_weight, down_weight)
    )

    def array(*shape):
        return jax.ShapeDtypeStruct(shape, BF16)

    def plane(rows):
        return array(rows, count, channels)

    dense_shape = array(channels // LANES, 5, 6 * LANES, 2 * LANES)
    up_shape, down_shape = array(*expand_weight.shape[1:]), array(*down_weight.shape[1:])
    half = extent // 2
    front, back = half + MARGIN, half - MARGIN

    def scratch(chunks, copies=0):
        return mix_scratch(chunks, count, channels, wide) + [pltpu.SemaphoreType.DMA((copies,))] * (copies > 0)

    chunks = split(front // 2)
    mixed_a, rows, taps, up, down, gain, dense = call(
        functools.partial(first_a_kernel, chunks), "first_a",
        [plane(front), plane(extent), array(*plane_weight.shape), up_shape, down_shape, array(*norm_gain.shape), dense_shape],
        (volume, plane_weight, expand_weight, down_weight, norm_gain), [HBM] * 5, scratch(chunks, 7), front // 2,
    )
    got_a = exchanged(mixed_a, reaches[0])
    chunks = split(back // 2)
    mixed_b, up_next, down_next, dense_next = call(
        functools.partial(first_b_kernel, chunks), "first_b", [plane(back), up_shape, down_shape, dense_shape],
        (rows, taps, up, down, gain, dense, expand_weight, down_weight), [VMEM] * 6 + [HBM] * 2,
        scratch(chunks, 2), back // 2,
    )
    got_b = exchanged(mixed_b, reaches[0])
    shared = (up_next, down_next, gain, dense_next, depth_weight)
    chunks = split(half // 2)
    current_a, wide_a = call(
        functools.partial(second_a_kernel, chunks, reaches[0]), "second_a", [plane(front), plane(half)],
        (rows, mixed_a, *got_a, *shared), [VMEM] * 9, scratch(chunks), half // 2,
    )
    far_a = exchanged(wide_a, reaches[1])
    current_b, wide_b = call(
        functools.partial(second_b_kernel, chunks, reaches[0]), "second_b", [plane(back), plane(half)],
        (rows, current_a, mixed_b, *got_b, *shared), [VMEM] * 10, scratch(chunks), half // 2,
    )
    far_b = exchanged(wide_b, reaches[1])
    features = final(
        functools.partial(final_a_kernel, reaches[1]), "final_a", volume.shape, half, {},
        depth_weight, current_a, wide_a, *far_a,
    )
    return final(
        functools.partial(final_b_kernel, reaches[1]), "final_b", volume.shape, half, {6: 0},
        depth_weight, current_a, current_b, wide_b, *far_b, features,
    )


def solution(mesh):
    placed = (P(("parts", "slab"), None, None, None), P(), P(), P(), P(), P())
    return jax.shard_map(
        shards,
        mesh=mesh,
        in_specs=placed,
        out_specs=P(("parts", "slab"), None, None, None),
        check_vma=False,
    )
```

```python
import functools

import jax
import jax.numpy as jnp
from jax import lax
from jax.experimental import pallas as pl
from jax.experimental.pallas import tpu as pltpu
from jax.sharding import PartitionSpec as P

FIRST_DILATION = 1
SECOND_DILATION = 4
EPSILON = 1e-06
LANES = 128
MARGIN = 2
FINAL_FLOPS = 1 << 34
LEAD = 6
TILE_FLOPS = 2 * 64 * 256 * (3840 + 2 * 1024)

BF16 = jnp.bfloat16
F32 = jnp.float32
VMEM = pl.BlockSpec(memory_space=pltpu.VMEM)
HBM = pl.BlockSpec(memory_space=pltpu.HBM)


def swapped(block, pairs):
    parts, size = lax.axis_size("parts"), lax.axis_size("slab")
    partner = {}
    for a, b in pairs:
        partner[a], partner[b] = b, a
    routes = []
    for part in range(parts):
        for i in range(size):
            if i in partner:
                routes.append((part * size + i, part * size + partner[i]))
            elif (part ^ 1) < parts:
                routes.append((part * size + i, (part ^ 1) * size + i))
    return lax.ppermute(block, ("parts", "slab"), routes)


def exchanged(block, reach):
    size = lax.axis_size("slab")
    return [swapped(block, [(i, i + reach) for i in range(size - reach) if i // reach % 2 == odd]) for odd in range(2)]


def ordered_coeffs(coeffs, reach):
    place = lax.axis_index("slab")
    even = lax.rem(lax.div(place, reach), 2) == 0
    below = jnp.where(place >= reach, coeffs[0:1], 0.0)
    above = jnp.where(place + reach < lax.axis_size("slab"), coeffs[2:3], 0.0)
    return jnp.where(even, above, below), coeffs[1:2], jnp.where(even, below, above)


def combined(base, own, first, second, coeffs):
    tap_first, tap_own, tap_second = coeffs
    term = tap_first * first.astype(F32) + tap_own * own.astype(F32) + tap_second * second.astype(F32)
    return (base.astype(F32) + term.astype(BF16).astype(F32)).astype(BF16)


def build_taps(taps, dense):
    group = taps.shape[2]
    lane_group = lax.broadcasted_iota(jnp.int32, (group, LANES), 1) // group

    for dy in range(5):
        for half in range(dense.shape[0]):
            lanes = slice(half * LANES, (half + 1) * LANES)
            for dx in range(5):
                tap = taps[dx, dy, :, lanes]
                for k in range(LANES // group):
                    value = jnp.where(lane_group == k, tap, jnp.zeros_like(tap))
                    for out in range(2):
                        row = (dx + out) * LANES + k * group
                        dense[half, dy, row : row + group, out * LANES : (out + 1) * LANES] = value
            for cell, out in ((5, 0), (0, 1)):
                rows = slice(cell * LANES, (cell + 1) * LANES)
                dense[half, dy, rows, out * LANES : (out + 1) * LANES] = jnp.zeros((LANES, LANES), BF16)


def fill_shifts(row, x, shifted):
    count = row.shape[0]
    position = lax.broadcasted_iota(jnp.int32, row.shape, 0)
    for dy in range(5):
        step = dy - 2
        value = row
        if step:
            value = pltpu.roll(row, -step % count, 0)
            keep = position < count - step if step > 0 else position >= -step
            value = jnp.where(keep, value, 0.0)
        shifted[dy, x // 2, x % 2] = value.astype(BF16)


def clear_row(x, shifted):
    shifted[:, x // 2, x % 2] = jnp.zeros((5,) + shifted.shape[3:], BF16)


def conv_normed(first_pair, pairs, shifted, dense, gain, normed):
    count, width = shifted.shape[3], shifted.shape[4]
    sums = []
    for half in range(width // LANES):
        lanes = slice(half * LANES, (half + 1) * LANES)
        total = None
        for dy in range(5):
            pieces = [
                shifted[dy, first_pair + block : first_pair + block + pairs, i, :, lanes].reshape(pairs * count, LANES)
                for block in range(3)
                for i in range(2)
            ]
            part = jnp.dot(jnp.concatenate(pieces, axis=-1), dense[half, dy], preferred_element_type=F32)
            total = part if total is None else total + part
        sums.append(total)
    for out in range(2):
        parts = [total[:, out * LANES : (out + 1) * LANES] for total in sums]
        squares = sum(part * part for part in parts)
        scale = lax.rsqrt(jnp.sum(squares, axis=-1, keepdims=True) / width + EPSILON)
        value = jnp.concatenate([part * scale for part in parts], axis=-1) * gain
        normed[:pairs, out] = value.astype(BF16).reshape(pairs, count, width)


def silu(value):
    half = 0.5 * value
    return half + half * jnp.tanh(half)


def mlp(rows, up, down, hidden):
    for start in range(0, up.shape[1], 256):
        value = jnp.dot(rows, up[:, start : start + 256], preferred_element_type=F32)
        hidden[:, start : start + 256] = silu(value).astype(BF16)
    return jnp.dot(hidden[...], down[...], preferred_element_type=F32).astype(BF16)


def mix(chunks, shifted, dense, gain, up, down, normed, hidden, mixed, copies=()):
    count, channels = shifted.shape[3:]
    starts = [sum(chunks[:k]) for k in range(len(chunks))]
    for k in range(len(chunks) + 1):
        if k < len(chunks):
            conv_normed(starts[k], chunks[k], shifted, dense, gain, normed.at[k % 2])
        if k == 1:
            for copy in copies:
                copy.wait()
        if k > 0:
            pairs, first = chunks[k - 1], starts[k - 1]
            rows = normed[(k - 1) % 2, :pairs].reshape(pairs * 2 * count, channels)
            result = mlp(rows, up, down, hidden.at[(k - 1) % 2, : pairs * 2 * count])
            mixed[first * 2 : (first + pairs) * 2] = result.reshape(pairs * 2, count, channels)


def call(body, name, outputs, inputs, in_specs, scratch, pairs=0):
    return pl.pallas_call(
        body,
        out_shape=outputs,
        in_specs=in_specs,
        out_specs=[VMEM] * len(outputs),
        scratch_shapes=scratch,
        compiler_params=pltpu.CompilerParams(vmem_limit_bytes=24 << 20),
        cost_estimate=pl.CostEstimate(flops=max(1, pairs) * 4 * TILE_FLOPS, bytes_accessed=1 << 20, transcendentals=0),
        name=name,
    )(*inputs)


def split(pairs):
    return (pairs,)


def mix_scratch(chunks, count, channels, wide):
    most = max(chunks)
    return [
        pltpu.VMEM((5, sum(chunks) + 2, 2, count, channels), BF16),
        pltpu.VMEM((2, most, 2, count, channels), BF16),
        pltpu.VMEM((2, most * 2 * count, wide), BF16),
    ]


def in_hbm(array):
    return pltpu.with_memory_space_constraint(array, pltpu.HBM)


def copies_in(pairs, sems):
    copies = [pltpu.make_async_copy(source, target, sems.at[k]) for k, (source, target) in enumerate(pairs)]
    for copy in copies:
        copy.start()
    return copies


def first_a_kernel(chunks, volume, taps_hbm, up_hbm, down_hbm, gain_hbm, mixed, rows, taps, up, down, gain, dense, shifted, normed, hidden, sems):
    front = shifted.shape[1] * 2 - MARGIN
    copies = copies_in(
        (
            (taps_hbm.at[0], taps.at[0]),
            (volume.at[0, :front], rows.at[:front]),
            (gain_hbm, gain),
            (up_hbm.at[0], up),
            (down_hbm.at[0], down),
            (volume.at[0, front:], rows.at[front:]),
            (taps_hbm.at[1], taps.at[1]),
        ),
        sems,
    )
    clear_row(0, shifted)
    clear_row(1, shifted)
    copies[0].wait()
    build_taps(taps.at[0], dense)
    copies[1].wait()
    for x in range(front):
        fill_shifts(rows[x].astype(F32), x + MARGIN, shifted)
    copies[2].wait()
    mix(chunks, shifted, dense, gain[0:1].astype(F32), up, down, normed, hidden, mixed, copies[3:5])
    copies[5].wait()
    copies[6].wait()


def first_b_kernel(chunks, rows, taps, up, down, gain, dense, up_hbm, down_hbm, mixed, up_next, down_next, dense_next, shifted, normed, hidden, sems):
    copies = copies_in(((up_hbm.at[1], up_next), (down_hbm.at[1], down_next)), sems)
    filled = shifted.shape[1] * 2 - MARGIN
    clear_row(filled, shifted)
    clear_row(filled + 1, shifted)
    for x in range(filled):
        fill_shifts(rows[rows.shape[0] - filled + x].astype(F32), x, shifted)
    mix(chunks, shifted, dense, gain[0:1].astype(F32), up, down, normed, hidden, mixed)
    build_taps(taps.at[1], dense_next)
    for copy in copies:
        copy.wait()


def second_a_kernel(chunks, reach, rows, own, first, second, up, down, gain, dense, coeffs, current, mixed, shifted, normed, hidden):
    clear_row(0, shifted)
    clear_row(1, shifted)
    taps = ordered_coeffs(coeffs[0].astype(F32), reach)
    for x in range(own.shape[0]):
        row = combined(rows[x], own[x], first[x], second[x], taps)
        current[x] = row
        fill_shifts(row.astype(F32), x + MARGIN, shifted)
    mix(chunks, shifted, dense, gain[1:2].astype(F32), up, down, normed, hidden, mixed)


def second_b_kernel(chunks, reach, rows, current_a, own, first, second, up, down, gain, dense, coeffs, current, mixed, shifted, normed, hidden):
    filled = shifted.shape[1] * 2
    clear_row(filled - 2, shifted)
    clear_row(filled - 1, shifted)
    before = filled - MARGIN - own.shape[0]
    for x in range(before):
        fill_shifts(current_a[current_a.shape[0] - before + x].astype(F32), x, shifted)
    taps = ordered_coeffs(coeffs[0].astype(F32), reach)
    for x in range(own.shape[0]):
        row = combined(rows[current_a.shape[0] + x], own[x], first[x], second[x], taps)
        current[x] = row
        fill_shifts(row.astype(F32), before + x, shifted)
    mix(chunks, shifted, dense, gain[1:2].astype(F32), up, down, normed, hidden, mixed)


def final_a_kernel(reach, coeff_ref, current, own, first, second, out, rows, sem):
    finish(reach, coeff_ref, [current[x] for x in range(rows.shape[0])], own, first, second, out, rows, sem, 0)


def final_b_kernel(reach, coeff_ref, current_a, current_b, own, first, second, before, out, rows, sem):
    kept = current_a.shape[0] + current_b.shape[0] - rows.shape[0]
    bases = [current_a[x] for x in range(kept, current_a.shape[0])] + [current_b[x] for x in range(current_b.shape[0])]
    finish(reach, coeff_ref, bases, own, first, second, out, rows, sem, kept)


def finish(reach, coeff_ref, bases, own, first, second, out, rows, sem, start):
    coeffs = ordered_coeffs(coeff_ref[1].astype(F32), reach)
    for x, base in enumerate(bases):
        rows[x] = combined(base, own[x], first[x], second[x], coeffs)
    copy = pltpu.make_async_copy(rows, out.at[0, start : start + rows.shape[0]], sem)
    copy.start()
    copy.wait()


def final(body, name, shape, rows, aliases, *inputs):
    return pl.pallas_call(
        body,
        out_shape=pltpu.HBM(shape, BF16),
        in_specs=[VMEM] * (len(inputs) - len(aliases)) + [HBM] * len(aliases),
        out_specs=HBM,
        scratch_shapes=[pltpu.VMEM((rows,) + shape[2:], BF16), pltpu.SemaphoreType.DMA],
        input_output_aliases=aliases,
        compiler_params=pltpu.CompilerParams(vmem_limit_bytes=8 << 20),
        cost_estimate=pl.CostEstimate(flops=FINAL_FLOPS, bytes_accessed=1024, transcendentals=0),
        name=name,
    )(*inputs)


def shards(volume, plane_weight, norm_gain, expand_weight, down_weight, depth_weight):
    depth, extent, count, channels = volume.shape
    wide = expand_weight.shape[2]
    reaches = (FIRST_DILATION // depth, SECOND_DILATION // depth)
    volume, plane_weight, norm_gain, expand_weight, down_weight = map(
        in_hbm, (volume, plane_weight, norm_gain, expand_weight, down_weight)
    )

    def array(*shape):
        return jax.ShapeDtypeStruct(shape, BF16)

    def plane(rows):
        return array(rows, count, channels)

    dense_shape = array(channels // LANES, 5, 6 * LANES, 2 * LANES)
    up_shape, down_shape = array(*expand_weight.shape[1:]), array(*down_weight.shape[1:])
    lead, rest = LEAD, extent - LEAD
    front, back = lead + MARGIN, rest - MARGIN

    def scratch(chunks, copies=0):
        return mix_scratch(chunks, count, channels, wide) + [pltpu.SemaphoreType.DMA((copies,))] * (copies > 0)

    chunks = split(front // 2)
    mixed_a, rows, taps, up, down, gain, dense = call(
        functools.partial(first_a_kernel, chunks), "first_a",
        [plane(front), plane(extent), array(*plane_weight.shape), up_shape, down_shape, array(*norm_gain.shape), dense_shape],
        (volume, plane_weight, expand_weight, down_weight, norm_gain), [HBM] * 5, scratch(chunks, 7), front // 2,
    )
    got_a = exchanged(mixed_a, reaches[0])
    chunks = split(back // 2)
    mixed_b, up_next, down_next, dense_next = call(
        functools.partial(first_b_kernel, chunks), "first_b", [plane(back), up_shape, down_shape, dense_shape],
        (rows, taps, up, down, gain, dense, expand_weight, down_weight), [VMEM] * 6 + [HBM] * 2,
        scratch(chunks, 2), back // 2,
    )
    got_b = exchanged(mixed_b, reaches[0])
    shared = (up_next, down_next, gain, dense_next, depth_weight)
    chunks = split(lead // 2)
    current_a, wide_a = call(
        functools.partial(second_a_kernel, chunks, reaches[0]), "second_a", [plane(front), plane(lead)],
        (rows, mixed_a, *got_a, *shared), [VMEM] * 9, scratch(chunks), lead // 2,
    )
    far_a = exchanged(wide_a, reaches[1])
    chunks = split(rest // 2)
    current_b, wide_b = call(
        functools.partial(second_b_kernel, chunks, reaches[0]), "second_b", [plane(back), plane(rest)],
        (rows, current_a, mixed_b, *got_b, *shared), [VMEM] * 10, scratch(chunks), rest // 2,
    )
    far_b = exchanged(wide_b, reaches[1])
    features = final(
        functools.partial(final_a_kernel, reaches[1]), "final_a", volume.shape, lead, {},
        depth_weight, current_a, wide_a, *far_a,
    )
    return final(
        functools.partial(final_b_kernel, reaches[1]), "final_b", volume.shape, rest, {6: 0},
        depth_weight, current_a, current_b, wide_b, *far_b, features,
    )


def solution(mesh):
    placed = (P(("parts", "slab"), None, None, None), P(), P(), P(), P(), P())
    return jax.shard_map(
        shards,
        mesh=mesh,
        in_specs=placed,
        out_specs=P(("parts", "slab"), None, None, None),
        check_vma=False,
    )
```

```python
import functools

import jax
import jax.numpy as jnp
from jax import lax
from jax.experimental import pallas as pl
from jax.experimental.pallas import tpu as pltpu
from jax.sharding import PartitionSpec as P

FIRST_DILATION = 1
SECOND_DILATION = 4
EPSILON = 1e-06
LANES = 128
MARGIN = 2
FINAL_FLOPS = 1 << 34
LEAD = 6
TILE_FLOPS = 2 * 64 * 256 * (3840 + 2 * 1024)

BF16 = jnp.bfloat16
F32 = jnp.float32
VMEM = pl.BlockSpec(memory_space=pltpu.VMEM)
HBM = pl.BlockSpec(memory_space=pltpu.HBM)


def swapped(block, pairs):
    parts, size = lax.axis_size("parts"), lax.axis_size("slab")
    partner = {}
    for a, b in pairs:
        partner[a], partner[b] = b, a
    for i in range(0, size - 1, 2):
        if i not in partner and i + 1 not in partner:
            partner[i], partner[i + 1] = i + 1, i
    routes = []
    for part in range(parts):
        for i in range(size):
            if i in partner:
                routes.append((part * size + i, part * size + partner[i]))
            elif (part ^ 1) < parts:
                routes.append((part * size + i, (part ^ 1) * size + i))
    return lax.ppermute(block, ("parts", "slab"), routes)


def exchanged(block, reach):
    size = lax.axis_size("slab")
    return [swapped(block, [(i, i + reach) for i in range(size - reach) if i // reach % 2 == odd]) for odd in range(2)]


def ordered_coeffs(coeffs, reach):
    place = lax.axis_index("slab")
    even = lax.rem(lax.div(place, reach), 2) == 0
    below = jnp.where(place >= reach, coeffs[0:1], 0.0)
    above = jnp.where(place + reach < lax.axis_size("slab"), coeffs[2:3], 0.0)
    return jnp.where(even, above, below), coeffs[1:2], jnp.where(even, below, above)


def combined(base, own, first, second, coeffs):
    tap_first, tap_own, tap_second = coeffs
    term = tap_first * first.astype(F32) + tap_own * own.astype(F32) + tap_second * second.astype(F32)
    return (base.astype(F32) + term.astype(BF16).astype(F32)).astype(BF16)


def build_taps(taps, dense):
    group = taps.shape[2]
    lane_group = lax.broadcasted_iota(jnp.int32, (group, LANES), 1) // group

    for dy in range(5):
        for half in range(dense.shape[0]):
            lanes = slice(half * LANES, (half + 1) * LANES)
            for dx in range(5):
                tap = taps[dx, dy, :, lanes]
                for k in range(LANES // group):
                    value = jnp.where(lane_group == k, tap, jnp.zeros_like(tap))
                    for out in range(2):
                        row = (dx + out) * LANES + k * group
                        dense[half, dy, row : row + group, out * LANES : (out + 1) * LANES] = value
            for cell, out in ((5, 0), (0, 1)):
                rows = slice(cell * LANES, (cell + 1) * LANES)
                dense[half, dy, rows, out * LANES : (out + 1) * LANES] = jnp.zeros((LANES, LANES), BF16)


def fill_shifts(row, x, shifted):
    count = row.shape[0]
    position = lax.broadcasted_iota(jnp.int32, row.shape, 0)
    for dy in range(5):
        step = dy - 2
        value = row
        if step:
            value = pltpu.roll(row, -step % count, 0)
            keep = position < count - step if step > 0 else position >= -step
            value = jnp.where(keep, value, 0.0)
        shifted[dy, x // 2, x % 2] = value.astype(BF16)


def clear_row(x, shifted):
    shifted[:, x // 2, x % 2] = jnp.zeros((5,) + shifted.shape[3:], BF16)


def conv_normed(first_pair, pairs, shifted, dense, gain, normed):
    count, width = shifted.shape[3], shifted.shape[4]
    sums = []
    for half in range(width // LANES):
        lanes = slice(half * LANES, (half + 1) * LANES)
        total = None
        for dy in range(5):
            pieces = [
                shifted[dy, first_pair + block : first_pair + block + pairs, i, :, lanes].reshape(pairs * count, LANES)
                for block in range(3)
                for i in range(2)
            ]
            part = jnp.dot(jnp.concatenate(pieces, axis=-1), dense[half, dy], preferred_element_type=F32)
            total = part if total is None else total + part
        sums.append(total)
    for out in range(2):
        parts = [total[:, out * LANES : (out + 1) * LANES] for total in sums]
        squares = sum(part * part for part in parts)
        scale = lax.rsqrt(jnp.sum(squares, axis=-1, keepdims=True) / width + EPSILON)
        value = jnp.concatenate([part * scale for part in parts], axis=-1) * gain
        normed[:pairs, out] = value.astype(BF16).reshape(pairs, count, width)


def silu(value):
    half = 0.5 * value
    return half + half * jnp.tanh(half)


def mlp(rows, up, down, hidden):
    for start in range(0, up.shape[1], 256):
        value = jnp.dot(rows, up[:, start : start + 256], preferred_element_type=F32)
        hidden[:, start : start + 256] = silu(value).astype(BF16)
    return jnp.dot(hidden[...], down[...], preferred_element_type=F32).astype(BF16)


def mix(chunks, shifted, dense, gain, up, down, normed, hidden, mixed, copies=()):
    count, channels = shifted.shape[3:]
    starts = [sum(chunks[:k]) for k in range(len(chunks))]
    for k in range(len(chunks) + 1):
        if k < len(chunks):
            conv_normed(starts[k], chunks[k], shifted, dense, gain, normed.at[k % 2])
        if k == 1:
            for copy in copies:
                copy.wait()
        if k > 0:
            pairs, first = chunks[k - 1], starts[k - 1]
            rows = normed[(k - 1) % 2, :pairs].reshape(pairs * 2 * count, channels)
            result = mlp(rows, up, down, hidden.at[(k - 1) % 2, : pairs * 2 * count])
            mixed[first * 2 : (first + pairs) * 2] = result.reshape(pairs * 2, count, channels)


def call(body, name, outputs, inputs, in_specs, scratch, pairs=0):
    return pl.pallas_call(
        body,
        out_shape=outputs,
        in_specs=in_specs,
        out_specs=[VMEM] * len(outputs),
        scratch_shapes=scratch,
        compiler_params=pltpu.CompilerParams(vmem_limit_bytes=24 << 20),
        cost_estimate=pl.CostEstimate(flops=max(1, pairs) * 4 * TILE_FLOPS, bytes_accessed=1 << 20, transcendentals=0),
        name=name,
    )(*inputs)


def split(pairs):
    return (pairs,)


def mix_scratch(chunks, count, channels, wide):
    most = max(chunks)
    return [
        pltpu.VMEM((5, sum(chunks) + 2, 2, count, channels), BF16),
        pltpu.VMEM((2, most, 2, count, channels), BF16),
        pltpu.VMEM((2, most * 2 * count, wide), BF16),
    ]


def in_hbm(array):
    return pltpu.with_memory_space_constraint(array, pltpu.HBM)


def copies_in(pairs, sems):
    copies = [pltpu.make_async_copy(source, target, sems.at[k]) for k, (source, target) in enumerate(pairs)]
    for copy in copies:
        copy.start()
    return copies


def first_a_kernel(chunks, volume, taps_hbm, up_hbm, down_hbm, gain_hbm, mixed, rows, taps, up, down, gain, dense, shifted, normed, hidden, sems):
    front = shifted.shape[1] * 2 - MARGIN
    copies = copies_in(
        (
            (taps_hbm.at[0], taps.at[0]),
            (volume.at[0, :front], rows.at[:front]),
            (gain_hbm, gain),
            (up_hbm.at[0], up),
            (down_hbm.at[0], down),
            (volume.at[0, front:], rows.at[front:]),
            (taps_hbm.at[1], taps.at[1]),
        ),
        sems,
    )
    clear_row(0, shifted)
    clear_row(1, shifted)
    copies[0].wait()
    build_taps(taps.at[0], dense)
    copies[1].wait()
    for x in range(front):
        fill_shifts(rows[x].astype(F32), x + MARGIN, shifted)
    copies[2].wait()
    mix(chunks, shifted, dense, gain[0:1].astype(F32), up, down, normed, hidden, mixed, copies[3:5])
    copies[5].wait()
    copies[6].wait()


def first_b_kernel(chunks, rows, taps, up, down, gain, dense, up_hbm, down_hbm, mixed, up_next, down_next, dense_next, shifted, normed, hidden, sems):
    copies = copies_in(((up_hbm.at[1], up_next), (down_hbm.at[1], down_next)), sems)
    filled = shifted.shape[1] * 2 - MARGIN
    clear_row(filled, shifted)
    clear_row(filled + 1, shifted)
    for x in range(filled):
        fill_shifts(rows[rows.shape[0] - filled + x].astype(F32), x, shifted)
    mix(chunks, shifted, dense, gain[0:1].astype(F32), up, down, normed, hidden, mixed)
    build_taps(taps.at[1], dense_next)
    for copy in copies:
        copy.wait()


def second_a_kernel(chunks, reach, rows, own, second, first, up, down, gain, dense, coeffs, current, mixed, shifted, normed, hidden):
    clear_row(0, shifted)
    clear_row(1, shifted)
    taps = ordered_coeffs(coeffs[0].astype(F32), reach)
    for x in range(own.shape[0]):
        row = combined(rows[x], own[x], first[x], second[x], taps)
        current[x] = row
        fill_shifts(row.astype(F32), x + MARGIN, shifted)
    mix(chunks, shifted, dense, gain[1:2].astype(F32), up, down, normed, hidden, mixed)


def second_b_kernel(chunks, reach, rows, current_a, own, second, first, up, down, gain, dense, coeffs, current, mixed, shifted, normed, hidden):
    filled = shifted.shape[1] * 2
    clear_row(filled - 2, shifted)
    clear_row(filled - 1, shifted)
    before = filled - MARGIN - own.shape[0]
    for x in range(before):
        fill_shifts(current_a[current_a.shape[0] - before + x].astype(F32), x, shifted)
    taps = ordered_coeffs(coeffs[0].astype(F32), reach)
    for x in range(own.shape[0]):
        row = combined(rows[current_a.shape[0] + x], own[x], first[x], second[x], taps)
        current[x] = row
        fill_shifts(row.astype(F32), before + x, shifted)
    mix(chunks, shifted, dense, gain[1:2].astype(F32), up, down, normed, hidden, mixed)


def final_a_kernel(reach, coeff_ref, current, own, second, first, out, rows, sem):
    finish(reach, coeff_ref, [current[x] for x in range(rows.shape[0])], own, first, second, out, rows, sem, 0)


def final_b_kernel(reach, coeff_ref, current_a, current_b, own, first, second, before, out, rows, sem):
    kept = current_a.shape[0] + current_b.shape[0] - rows.shape[0]
    bases = [current_a[x] for x in range(kept, current_a.shape[0])] + [current_b[x] for x in range(current_b.shape[0])]
    finish(reach, coeff_ref, bases, own, first, second, out, rows, sem, kept)


def finish(reach, coeff_ref, bases, own, first, second, out, rows, sem, start):
    coeffs = ordered_coeffs(coeff_ref[1].astype(F32), reach)
    for x, base in enumerate(bases):
        rows[x] = combined(base, own[x], first[x], second[x], coeffs)
    copy = pltpu.make_async_copy(rows, out.at[0, start : start + rows.shape[0]], sem)
    copy.start()
    copy.wait()


def final(body, name, shape, rows, aliases, *inputs):
    return pl.pallas_call(
        body,
        out_shape=pltpu.HBM(shape, BF16),
        in_specs=[VMEM] * (len(inputs) - len(aliases)) + [HBM] * len(aliases),
        out_specs=HBM,
        scratch_shapes=[pltpu.VMEM((rows,) + shape[2:], BF16), pltpu.SemaphoreType.DMA],
        input_output_aliases=aliases,
        compiler_params=pltpu.CompilerParams(vmem_limit_bytes=8 << 20),
        cost_estimate=pl.CostEstimate(flops=FINAL_FLOPS, bytes_accessed=1024, transcendentals=0),
        name=name,
    )(*inputs)


def shards(volume, plane_weight, norm_gain, expand_weight, down_weight, depth_weight):
    depth, extent, count, channels = volume.shape
    wide = expand_weight.shape[2]
    reaches = (FIRST_DILATION // depth, SECOND_DILATION // depth)
    volume, plane_weight, norm_gain, expand_weight, down_weight = map(
        in_hbm, (volume, plane_weight, norm_gain, expand_weight, down_weight)
    )

    def array(*shape):
        return jax.ShapeDtypeStruct(shape, BF16)

    def plane(rows):
        return array(rows, count, channels)

    dense_shape = array(channels // LANES, 5, 6 * LANES, 2 * LANES)
    up_shape, down_shape = array(*expand_weight.shape[1:]), array(*down_weight.shape[1:])
    lead, rest = LEAD, extent - LEAD
    front, back = lead + MARGIN, rest - MARGIN

    def scratch(chunks, copies=0):
        return mix_scratch(chunks, count, channels, wide) + [pltpu.SemaphoreType.DMA((copies,))] * (copies > 0)

    chunks = split(front // 2)
    mixed_a, rows, taps, up, down, gain, dense = call(
        functools.partial(first_a_kernel, chunks), "first_a",
        [plane(front), plane(extent), array(*plane_weight.shape), up_shape, down_shape, array(*norm_gain.shape), dense_shape],
        (volume, plane_weight, expand_weight, down_weight, norm_gain), [HBM] * 5, scratch(chunks, 7), front // 2,
    )
    got_a = exchanged(mixed_a, reaches[0])
    chunks = split(back // 2)
    mixed_b, up_next, down_next, dense_next = call(
        functools.partial(first_b_kernel, chunks), "first_b", [plane(back), up_shape, down_shape, dense_shape],
        (rows, taps, up, down, gain, dense, expand_weight, down_weight), [VMEM] * 6 + [HBM] * 2,
        scratch(chunks, 2), back // 2,
    )
    got_b = exchanged(mixed_b, reaches[0])
    shared = (up_next, down_next, gain, dense_next, depth_weight)
    chunks = split(lead // 2)
    current_a, wide_a = call(
        functools.partial(second_a_kernel, chunks, reaches[0]), "second_a", [plane(front), plane(lead)],
        (rows, mixed_a, *got_a[::-1], *shared), [VMEM] * 9, scratch(chunks), lead // 2,
    )
    far_a = exchanged(wide_a, reaches[1])
    chunks = split(rest // 2)
    current_b, wide_b = call(
        functools.partial(second_b_kernel, chunks, reaches[0]), "second_b", [plane(back), plane(rest)],
        (rows, current_a, mixed_b, *got_b[::-1], *shared), [VMEM] * 10, scratch(chunks), rest // 2,
    )
    far_b = exchanged(wide_b, reaches[1])
    features = final(
        functools.partial(final_a_kernel, reaches[1]), "final_a", volume.shape, lead, {},
        depth_weight, current_a, wide_a, *far_a[::-1],
    )
    return final(
        functools.partial(final_b_kernel, reaches[1]), "final_b", volume.shape, rest, {6: 0},
        depth_weight, current_a, current_b, wide_b, *far_b, features,
    )


def solution(mesh):
    placed = (P(("parts", "slab"), None, None, None), P(), P(), P(), P(), P())
    return jax.shard_map(
        shards,
        mesh=mesh,
        in_specs=placed,
        out_specs=P(("parts", "slab"), None, None, None),
        check_vma=False,
    )
```

```python
import functools

import jax
import jax.numpy as jnp
from jax import lax
from jax.experimental import pallas as pl
from jax.experimental.pallas import tpu as pltpu
from jax.sharding import PartitionSpec as P

FIRST_DILATION = 1
SECOND_DILATION = 4
EPSILON = 1e-06
LANES = 128
MARGIN = 2
FINAL_FLOPS = 1 << 34
LEAD = 6
TILE_FLOPS = 2 * 64 * 256 * (3840 + 2 * 1024)

BF16 = jnp.bfloat16
F32 = jnp.float32
VMEM = pl.BlockSpec(memory_space=pltpu.VMEM)
HBM = pl.BlockSpec(memory_space=pltpu.HBM)


def swapped(block, pairs):
    parts, size = lax.axis_size("parts"), lax.axis_size("slab")
    partner = {}
    for a, b in pairs:
        partner[a], partner[b] = b, a
    for i in range(0, size - 1, 2):
        if i not in partner and i + 1 not in partner:
            partner[i], partner[i + 1] = i + 1, i
    routes = []
    for part in range(parts):
        for i in range(size):
            if i in partner:
                routes.append((part * size + i, part * size + partner[i]))
            elif (part ^ 1) < parts:
                routes.append((part * size + i, (part ^ 1) * size + i))
    return lax.ppermute(block, ("parts", "slab"), routes)


def exchanged(block, reach):
    size = lax.axis_size("slab")
    return [swapped(block, [(i, i + reach) for i in range(size - reach) if i // reach % 2 == odd]) for odd in range(2)]


def ordered_coeffs(coeffs, reach):
    place = lax.axis_index("slab")
    even = lax.rem(lax.div(place, reach), 2) == 0
    below = jnp.where(place >= reach, coeffs[0:1], 0.0)
    above = jnp.where(place + reach < lax.axis_size("slab"), coeffs[2:3], 0.0)
    return jnp.where(even, above, below), coeffs[1:2], jnp.where(even, below, above)


def combined(base, own, first, second, coeffs):
    tap_first, tap_own, tap_second = coeffs
    term = tap_first * first.astype(F32) + tap_own * own.astype(F32) + tap_second * second.astype(F32)
    return (base.astype(F32) + term.astype(BF16).astype(F32)).astype(BF16)


def build_taps(taps, dense):
    group = taps.shape[2]
    lane_group = lax.broadcasted_iota(jnp.int32, (group, LANES), 1) // group

    for dy in range(5):
        for half in range(dense.shape[0]):
            lanes = slice(half * LANES, (half + 1) * LANES)
            for dx in range(5):
                tap = taps[dx, dy, :, lanes]
                for k in range(LANES // group):
                    value = jnp.where(lane_group == k, tap, jnp.zeros_like(tap))
                    for out in range(2):
                        row = (dx + out) * LANES + k * group
                        dense[half, dy, row : row + group, out * LANES : (out + 1) * LANES] = value
            for cell, out in ((5, 0), (0, 1)):
                rows = slice(cell * LANES, (cell + 1) * LANES)
                dense[half, dy, rows, out * LANES : (out + 1) * LANES] = jnp.zeros((LANES, LANES), BF16)


def fill_shifts(row, x, shifted):
    count = row.shape[0]
    position = lax.broadcasted_iota(jnp.int32, row.shape, 0)
    for dy in range(5):
        step = dy - 2
        value = row
        if step:
            value = pltpu.roll(row, -step % count, 0)
            keep = position < count - step if step > 0 else position >= -step
            value = jnp.where(keep, value, 0.0)
        shifted[dy, x // 2, x % 2] = value.astype(BF16)


def clear_row(x, shifted):
    shifted[:, x // 2, x % 2] = jnp.zeros((5,) + shifted.shape[3:], BF16)


def conv_normed(first_pair, pairs, shifted, dense, gain, normed):
    count, width = shifted.shape[3], shifted.shape[4]
    sums = []
    for half in range(width // LANES):
        lanes = slice(half * LANES, (half + 1) * LANES)
        total = None
        for dy in range(5):
            pieces = [
                shifted[dy, first_pair + block : first_pair + block + pairs, i, :, lanes].reshape(pairs * count, LANES)
                for block in range(3)
                for i in range(2)
            ]
            part = jnp.dot(jnp.concatenate(pieces, axis=-1), dense[half, dy], preferred_element_type=F32)
            total = part if total is None else total + part
        sums.append(total)
    for out in range(2):
        parts = [total[:, out * LANES : (out + 1) * LANES] for total in sums]
        squares = sum(part * part for part in parts)
        scale = lax.rsqrt(jnp.sum(squares, axis=-1, keepdims=True) / width + EPSILON)
        value = jnp.concatenate([part * scale for part in parts], axis=-1) * gain
        normed[:pairs, out] = value.astype(BF16).reshape(pairs, count, width)


def silu(value):
    half = 0.5 * value
    return half + half * jnp.tanh(half)


def mlp(rows, up, down, hidden):
    for start in range(0, up.shape[1], 256):
        value = jnp.dot(rows, up[:, start : start + 256], preferred_element_type=F32)
        hidden[:, start : start + 256] = silu(value).astype(BF16)
    return jnp.dot(hidden[...], down[...], preferred_element_type=F32).astype(BF16)


def mix(chunks, shifted, dense, gain, up, down, normed, hidden, mixed, copies=()):
    count, channels = shifted.shape[3:]
    starts = [sum(chunks[:k]) for k in range(len(chunks))]
    for k in range(len(chunks) + 1):
        if k < len(chunks):
            conv_normed(starts[k], chunks[k], shifted, dense, gain, normed.at[k % 2])
        if k == 1:
            for copy in copies:
                copy.wait()
        if k > 0:
            pairs, first = chunks[k - 1], starts[k - 1]
            rows = normed[(k - 1) % 2, :pairs].reshape(pairs * 2 * count, channels)
            result = mlp(rows, up, down, hidden.at[(k - 1) % 2, : pairs * 2 * count])
            mixed[first * 2 : (first + pairs) * 2] = result.reshape(pairs * 2, count, channels)


def call(body, name, outputs, inputs, in_specs, scratch, pairs=0):
    return pl.pallas_call(
        body,
        out_shape=outputs,
        in_specs=in_specs,
        out_specs=[VMEM] * len(outputs),
        scratch_shapes=scratch,
        compiler_params=pltpu.CompilerParams(vmem_limit_bytes=24 << 20),
        cost_estimate=pl.CostEstimate(flops=max(1, pairs) * 4 * TILE_FLOPS, bytes_accessed=1 << 20, transcendentals=0),
        name=name,
    )(*inputs)


def split(pairs):
    return (pairs,)


def mix_scratch(chunks, count, channels, wide):
    most = max(chunks)
    return [
        pltpu.VMEM((5, sum(chunks) + 2, 2, count, channels), BF16),
        pltpu.VMEM((2, most, 2, count, channels), BF16),
        pltpu.VMEM((2, most * 2 * count, wide), BF16),
    ]


def in_hbm(array):
    return pltpu.with_memory_space_constraint(array, pltpu.HBM)


def copies_in(pairs, sems):
    copies = [pltpu.make_async_copy(source, target, sems.at[k]) for k, (source, target) in enumerate(pairs)]
    for copy in copies:
        copy.start()
    return copies


def first_a_kernel(chunks, volume, taps_hbm, up_hbm, down_hbm, gain_hbm, mixed, rows, taps, up, down, gain, dense, shifted, normed, hidden, sems):
    front = shifted.shape[1] * 2 - MARGIN
    copies = copies_in(
        (
            (taps_hbm.at[0], taps.at[0]),
            (volume.at[0, :front], rows.at[:front]),
            (gain_hbm, gain),
            (up_hbm.at[0], up),
            (down_hbm.at[0], down),
            (volume.at[0, front:], rows.at[front:]),
            (taps_hbm.at[1], taps.at[1]),
        ),
        sems,
    )
    clear_row(0, shifted)
    clear_row(1, shifted)
    copies[0].wait()
    build_taps(taps.at[0], dense)
    copies[1].wait()
    for x in range(front):
        fill_shifts(rows[x].astype(F32), x + MARGIN, shifted)
    copies[2].wait()
    mix(chunks, shifted, dense, gain[0:1].astype(F32), up, down, normed, hidden, mixed, copies[3:5])
    copies[5].wait()
    copies[6].wait()


def first_b_kernel(chunks, rows, taps, up, down, gain, dense, up_hbm, down_hbm, mixed, up_next, down_next, dense_next, shifted, normed, hidden, sems):
    copies = copies_in(((up_hbm.at[1], up_next), (down_hbm.at[1], down_next)), sems)
    filled = shifted.shape[1] * 2 - MARGIN
    clear_row(filled, shifted)
    clear_row(filled + 1, shifted)
    for x in range(filled):
        fill_shifts(rows[rows.shape[0] - filled + x].astype(F32), x, shifted)
    mix(chunks, shifted, dense, gain[0:1].astype(F32), up, down, normed, hidden, mixed)
    build_taps(taps.at[1], dense_next)
    for copy in copies:
        copy.wait()


def second_a_kernel(chunks, reach, rows, own, second, first, up, down, gain, dense, coeffs, current, mixed, shifted, normed, hidden):
    clear_row(0, shifted)
    clear_row(1, shifted)
    taps = ordered_coeffs(coeffs[0].astype(F32), reach)
    for x in range(own.shape[0]):
        row = combined(rows[x], own[x], first[x], second[x], taps)
        current[x] = row
        fill_shifts(row.astype(F32), x + MARGIN, shifted)
    mix(chunks, shifted, dense, gain[1:2].astype(F32), up, down, normed, hidden, mixed)


def second_b_kernel(chunks, reach, rows, current_a, own, second, first, up, down, gain, dense, coeffs, current, mixed, shifted, normed, hidden):
    filled = shifted.shape[1] * 2
    clear_row(filled - 2, shifted)
    clear_row(filled - 1, shifted)
    before = filled - MARGIN - own.shape[0]
    for x in range(before):
        fill_shifts(current_a[current_a.shape[0] - before + x].astype(F32), x, shifted)
    taps = ordered_coeffs(coeffs[0].astype(F32), reach)
    for x in range(own.shape[0]):
        row = combined(rows[current_a.shape[0] + x], own[x], first[x], second[x], taps)
        current[x] = row
        fill_shifts(row.astype(F32), before + x, shifted)
    mix(chunks, shifted, dense, gain[1:2].astype(F32), up, down, normed, hidden, mixed)


def final_a_kernel(reach, coeff_ref, current, own, second, first, out, rows, sem):
    finish(reach, coeff_ref, [current[x] for x in range(rows.shape[0])], own, first, second, out, rows, sem, 0)


def final_b_kernel(reach, coeff_ref, current_a, current_b, own, first, second, before, out, rows, sem):
    kept = current_a.shape[0] + current_b.shape[0] - rows.shape[0]
    bases = [current_a[x] for x in range(kept, current_a.shape[0])] + [current_b[x] for x in range(current_b.shape[0])]
    finish(reach, coeff_ref, bases, own, first, second, out, rows, sem, kept)


def finish(reach, coeff_ref, bases, own, first, second, out, rows, sem, start):
    coeffs = ordered_coeffs(coeff_ref[1].astype(F32), reach)
    cut = len(bases) // 2
    copies = [
        pltpu.make_async_copy(rows.at[a:b], out.at[0, start + a : start + b], sem.at[k])
        for k, (a, b) in enumerate(((0, cut), (cut, len(bases))))
    ]
    for x, base in enumerate(bases):
        rows[x] = combined(base, own[x], first[x], second[x], coeffs)
        if x + 1 == cut:
            copies[0].start()
    copies[1].start()
    for copy in copies:
        copy.wait()


def final(body, name, shape, rows, aliases, *inputs):
    return pl.pallas_call(
        body,
        out_shape=pltpu.HBM(shape, BF16),
        in_specs=[VMEM] * (len(inputs) - len(aliases)) + [HBM] * len(aliases),
        out_specs=HBM,
        scratch_shapes=[pltpu.VMEM((rows,) + shape[2:], BF16), pltpu.SemaphoreType.DMA((2,))],
        input_output_aliases=aliases,
        compiler_params=pltpu.CompilerParams(vmem_limit_bytes=8 << 20),
        cost_estimate=pl.CostEstimate(flops=FINAL_FLOPS, bytes_accessed=1024, transcendentals=0),
        name=name,
    )(*inputs)


def shards(volume, plane_weight, norm_gain, expand_weight, down_weight, depth_weight):
    depth, extent, count, channels = volume.shape
    wide = expand_weight.shape[2]
    reaches = (FIRST_DILATION // depth, SECOND_DILATION // depth)
    volume, plane_weight, norm_gain, expand_weight, down_weight = map(
        in_hbm, (volume, plane_weight, norm_gain, expand_weight, down_weight)
    )

    def array(*shape):
        return jax.ShapeDtypeStruct(shape, BF16)

    def plane(rows):
        return array(rows, count, channels)

    dense_shape = array(channels // LANES, 5, 6 * LANES, 2 * LANES)
    up_shape, down_shape = array(*expand_weight.shape[1:]), array(*down_weight.shape[1:])
    lead, rest = LEAD, extent - LEAD
    front, back = lead + MARGIN, rest - MARGIN

    def scratch(chunks, copies=0):
        return mix_scratch(chunks, count, channels, wide) + [pltpu.SemaphoreType.DMA((copies,))] * (copies > 0)

    chunks = split(front // 2)
    mixed_a, rows, taps, up, down, gain, dense = call(
        functools.partial(first_a_kernel, chunks), "first_a",
        [plane(front), plane(extent), array(*plane_weight.shape), up_shape, down_shape, array(*norm_gain.shape), dense_shape],
        (volume, plane_weight, expand_weight, down_weight, norm_gain), [HBM] * 5, scratch(chunks, 7), front // 2,
    )
    got_a = exchanged(mixed_a, reaches[0])
    chunks = split(back // 2)
    mixed_b, up_next, down_next, dense_next = call(
        functools.partial(first_b_kernel, chunks), "first_b", [plane(back), up_shape, down_shape, dense_shape],
        (rows, taps, up, down, gain, dense, expand_weight, down_weight), [VMEM] * 6 + [HBM] * 2,
        scratch(chunks, 2), back // 2,
    )
    got_b = exchanged(mixed_b, reaches[0])
    shared = (up_next, down_next, gain, dense_next, depth_weight)
    chunks = split(lead // 2)
    current_a, wide_a = call(
        functools.partial(second_a_kernel, chunks, reaches[0]), "second_a", [plane(front), plane(lead)],
        (rows, mixed_a, *got_a[::-1], *shared), [VMEM] * 9, scratch(chunks), lead // 2,
    )
    far_a = exchanged(wide_a, reaches[1])
    chunks = split(rest // 2)
    current_b, wide_b = call(
        functools.partial(second_b_kernel, chunks, reaches[0]), "second_b", [plane(back), plane(rest)],
        (rows, current_a, mixed_b, *got_b[::-1], *shared), [VMEM] * 10, scratch(chunks), rest // 2,
    )
    far_b = exchanged(wide_b, reaches[1])
    features = final(
        functools.partial(final_a_kernel, reaches[1]), "final_a", volume.shape, lead, {},
        depth_weight, current_a, wide_a, *far_a[::-1],
    )
    return final(
        functools.partial(final_b_kernel, reaches[1]), "final_b", volume.shape, rest, {6: 0},
        depth_weight, current_a, current_b, wide_b, *far_b, features,
    )


def solution(mesh):
    placed = (P(("parts", "slab"), None, None, None), P(), P(), P(), P(), P())
    return jax.shard_map(
        shards,
        mesh=mesh,
        in_specs=placed,
        out_specs=P(("parts", "slab"), None, None, None),
        check_vma=False,
    )
```

```python
import functools

import jax
import jax.numpy as jnp
from jax import lax
from jax.experimental import pallas as pl
from jax.experimental.pallas import tpu as pltpu
from jax.sharding import PartitionSpec as P

FIRST_DILATION = 1
SECOND_DILATION = 4
EPSILON = 1e-06
LANES = 128
MARGIN = 2
FINAL_FLOPS = 1 << 34
LEAD = 6
TILE_FLOPS = 2 * 64 * 256 * (3840 + 2 * 1024)

BF16 = jnp.bfloat16
F32 = jnp.float32
VMEM = pl.BlockSpec(memory_space=pltpu.VMEM)
HBM = pl.BlockSpec(memory_space=pltpu.HBM)


def swapped(block, pairs):
    parts, size = lax.axis_size("parts"), lax.axis_size("slab")
    partner = {}
    for a, b in pairs:
        partner[a], partner[b] = b, a
    for i in range(0, size - 1, 2):
        if i not in partner and i + 1 not in partner:
            partner[i], partner[i + 1] = i + 1, i
    routes = []
    for part in range(parts):
        for i in range(size):
            if i in partner:
                routes.append((part * size + i, part * size + partner[i]))
            elif (part ^ 1) < parts:
                routes.append((part * size + i, (part ^ 1) * size + i))
    return lax.ppermute(block, ("parts", "slab"), routes)


def exchanged(block, reach):
    size = lax.axis_size("slab")
    return [swapped(block, [(i, i + reach) for i in range(size - reach) if i // reach % 2 == odd]) for odd in range(2)]


def ordered_coeffs(coeffs, reach):
    place = lax.axis_index("slab")
    even = lax.rem(lax.div(place, reach), 2) == 0
    below = jnp.where(place >= reach, coeffs[0:1], 0.0)
    above = jnp.where(place + reach < lax.axis_size("slab"), coeffs[2:3], 0.0)
    return jnp.where(even, above, below), coeffs[1:2], jnp.where(even, below, above)


def combined(base, own, first, second, coeffs):
    tap_first, tap_own, tap_second = coeffs
    term = tap_first * first.astype(F32) + tap_own * own.astype(F32) + tap_second * second.astype(F32)
    return (base.astype(F32) + term.astype(BF16).astype(F32)).astype(BF16)


def build_taps(taps, dense):
    group = taps.shape[2]
    lane_group = lax.broadcasted_iota(jnp.int32, (group, LANES), 1) // group

    for dy in range(5):
        for half in range(dense.shape[0]):
            lanes = slice(half * LANES, (half + 1) * LANES)
            for dx in range(5):
                tap = taps[dx, dy, :, lanes]
                for k in range(LANES // group):
                    value = jnp.where(lane_group == k, tap, jnp.zeros_like(tap))
                    for out in range(2):
                        row = (dx + out) * LANES + k * group
                        dense[half, dy, row : row + group, out * LANES : (out + 1) * LANES] = value
            for cell, out in ((5, 0), (0, 1)):
                rows = slice(cell * LANES, (cell + 1) * LANES)
                dense[half, dy, rows, out * LANES : (out + 1) * LANES] = jnp.zeros((LANES, LANES), BF16)


def fill_shifts(row, x, shifted):
    count = row.shape[0]
    position = lax.broadcasted_iota(jnp.int32, row.shape, 0)
    for dy in range(5):
        step = dy - 2
        value = row
        if step:
            value = pltpu.roll(row, -step % count, 0)
            keep = position < count - step if step > 0 else position >= -step
            value = jnp.where(keep, value, 0.0)
        shifted[dy, x // 2, x % 2] = value.astype(BF16)


def clear_row(x, shifted):
    shifted[:, x // 2, x % 2] = jnp.zeros((5,) + shifted.shape[3:], BF16)


def conv_normed(first_pair, pairs, shifted, dense, gain, normed):
    count, width = shifted.shape[3], shifted.shape[4]
    sums = []
    for half in range(width // LANES):
        lanes = slice(half * LANES, (half + 1) * LANES)
        total = None
        for dy in range(5):
            pieces = [
                shifted[dy, first_pair + block : first_pair + block + pairs, i, :, lanes].reshape(pairs * count, LANES)
                for block in range(3)
                for i in range(2)
            ]
            part = jnp.dot(jnp.concatenate(pieces, axis=-1), dense[half, dy], preferred_element_type=F32)
            total = part if total is None else total + part
        sums.append(total)
    for out in range(2):
        parts = [total[:, out * LANES : (out + 1) * LANES] for total in sums]
        squares = sum(part * part for part in parts)
        scale = lax.rsqrt(jnp.sum(squares, axis=-1, keepdims=True) / width + EPSILON)
        value = jnp.concatenate([part * scale for part in parts], axis=-1) * gain
        normed[:pairs, out] = value.astype(BF16).reshape(pairs, count, width)


def silu(value):
    half = 0.5 * value
    return half + half * jnp.tanh(half)


def mlp(rows, up, down, hidden):
    for start in range(0, up.shape[1], 256):
        value = jnp.dot(rows, up[:, start : start + 256], preferred_element_type=F32)
        hidden[:, start : start + 256] = silu(value).astype(BF16)
    return jnp.dot(hidden[...], down[...], preferred_element_type=F32).astype(BF16)


def mix(chunks, shifted, dense, gain, up, down, normed, hidden, mixed, copies=()):
    count, channels = shifted.shape[3:]
    starts = [sum(chunks[:k]) for k in range(len(chunks))]
    for k in range(len(chunks) + 1):
        if k < len(chunks):
            conv_normed(starts[k], chunks[k], shifted, dense, gain, normed.at[k % 2])
        if k == 1:
            for copy in copies:
                copy.wait()
        if k > 0:
            pairs, first = chunks[k - 1], starts[k - 1]
            rows = normed[(k - 1) % 2, :pairs].reshape(pairs * 2 * count, channels)
            result = mlp(rows, up, down, hidden.at[(k - 1) % 2, : pairs * 2 * count])
            mixed[first * 2 : (first + pairs) * 2] = result.reshape(pairs * 2, count, channels)


def call(body, name, outputs, inputs, in_specs, scratch, pairs=0):
    return pl.pallas_call(
        body,
        out_shape=outputs,
        in_specs=in_specs,
        out_specs=[VMEM] * len(outputs),
        scratch_shapes=scratch,
        compiler_params=pltpu.CompilerParams(vmem_limit_bytes=24 << 20),
        cost_estimate=pl.CostEstimate(flops=max(1, pairs) * 4 * TILE_FLOPS, bytes_accessed=1 << 20, transcendentals=0),
        name=name,
    )(*inputs)


def split(pairs):
    return (pairs,)


def mix_scratch(chunks, count, channels, wide):
    most = max(chunks)
    return [
        pltpu.VMEM((5, sum(chunks) + 2, 2, count, channels), BF16),
        pltpu.VMEM((2, most, 2, count, channels), BF16),
        pltpu.VMEM((2, most * 2 * count, wide), BF16),
    ]


def in_hbm(array):
    return pltpu.with_memory_space_constraint(array, pltpu.HBM)


def copies_in(pairs, sems):
    copies = [pltpu.make_async_copy(source, target, sems.at[k]) for k, (source, target) in enumerate(pairs)]
    for copy in copies:
        copy.start()
    return copies


def first_a_kernel(chunks, volume, taps_hbm, up_hbm, down_hbm, gain_hbm, mixed, rows, taps, up, down, gain, dense, shifted, normed, hidden, sems):
    front = shifted.shape[1] * 2 - MARGIN
    copies = copies_in(
        (
            (taps_hbm.at[0], taps.at[0]),
            (volume.at[0, :front], rows.at[:front]),
            (gain_hbm, gain),
            (up_hbm.at[0], up),
            (down_hbm.at[0], down),
            (volume.at[0, front:], rows.at[front:]),
            (taps_hbm.at[1], taps.at[1]),
        ),
        sems,
    )
    clear_row(0, shifted)
    clear_row(1, shifted)
    copies[0].wait()
    build_taps(taps.at[0], dense)
    copies[1].wait()
    for x in range(front):
        fill_shifts(rows[x].astype(F32), x + MARGIN, shifted)
    copies[2].wait()
    mix(chunks, shifted, dense, gain[0:1].astype(F32), up, down, normed, hidden, mixed, copies[3:5])
    copies[5].wait()
    copies[6].wait()


def first_b_kernel(chunks, rows, taps, up, down, gain, dense, up_hbm, down_hbm, mixed, up_next, down_next, dense_next, shifted, normed, hidden, sems):
    copies = copies_in(((up_hbm.at[1], up_next), (down_hbm.at[1], down_next)), sems)
    filled = shifted.shape[1] * 2 - MARGIN
    clear_row(filled, shifted)
    clear_row(filled + 1, shifted)
    for x in range(filled):
        fill_shifts(rows[rows.shape[0] - filled + x].astype(F32), x, shifted)
    build_taps(taps.at[1], dense_next)
    mix(chunks, shifted, dense, gain[0:1].astype(F32), up, down, normed, hidden, mixed)
    for copy in copies:
        copy.wait()


def second_a_kernel(chunks, reach, rows, own, second, first, up, down, gain, dense, coeffs, current, mixed, shifted, normed, hidden):
    clear_row(0, shifted)
    clear_row(1, shifted)
    taps = ordered_coeffs(coeffs[0].astype(F32), reach)
    for x in range(own.shape[0]):
        row = combined(rows[x], own[x], first[x], second[x], taps)
        current[x] = row
        fill_shifts(row.astype(F32), x + MARGIN, shifted)
    mix(chunks, shifted, dense, gain[1:2].astype(F32), up, down, normed, hidden, mixed)


def second_b_kernel(chunks, reach, rows, current_a, own, second, first, up, down, gain, dense, coeffs, current, mixed, shifted, normed, hidden):
    filled = shifted.shape[1] * 2
    clear_row(filled - 2, shifted)
    clear_row(filled - 1, shifted)
    before = filled - MARGIN - own.shape[0]
    for x in range(before):
        fill_shifts(current_a[current_a.shape[0] - before + x].astype(F32), x, shifted)
    taps = ordered_coeffs(coeffs[0].astype(F32), reach)
    for x in range(own.shape[0]):
        row = combined(rows[current_a.shape[0] + x], own[x], first[x], second[x], taps)
        current[x] = row
        fill_shifts(row.astype(F32), before + x, shifted)
    mix(chunks, shifted, dense, gain[1:2].astype(F32), up, down, normed, hidden, mixed)


def final_a_kernel(reach, coeff_ref, current, own, second, first, out, rows, sem):
    finish(reach, coeff_ref, [current[x] for x in range(rows.shape[0])], own, first, second, out, rows, sem, 0)


def final_b_kernel(reach, coeff_ref, current_a, current_b, own, first, second, before, out, rows, sem):
    kept = current_a.shape[0] + current_b.shape[0] - rows.shape[0]
    bases = [current_a[x] for x in range(kept, current_a.shape[0])] + [current_b[x] for x in range(current_b.shape[0])]
    finish(reach, coeff_ref, bases, own, first, second, out, rows, sem, kept)


def finish(reach, coeff_ref, bases, own, first, second, out, rows, sem, start):
    coeffs = ordered_coeffs(coeff_ref[1].astype(F32), reach)
    cut = len(bases) // 2
    copies = [
        pltpu.make_async_copy(rows.at[a:b], out.at[0, start + a : start + b], sem.at[k])
        for k, (a, b) in enumerate(((0, cut), (cut, len(bases))))
    ]
    for x, base in enumerate(bases):
        rows[x] = combined(base, own[x], first[x], second[x], coeffs)
        if x + 1 == cut:
            copies[0].start()
    copies[1].start()
    for copy in copies:
        copy.wait()


def final(body, name, shape, rows, aliases, *inputs):
    return pl.pallas_call(
        body,
        out_shape=pltpu.HBM(shape, BF16),
        in_specs=[VMEM] * (len(inputs) - len(aliases)) + [HBM] * len(aliases),
        out_specs=HBM,
        scratch_shapes=[pltpu.VMEM((rows,) + shape[2:], BF16), pltpu.SemaphoreType.DMA((2,))],
        input_output_aliases=aliases,
        compiler_params=pltpu.CompilerParams(vmem_limit_bytes=8 << 20),
        cost_estimate=pl.CostEstimate(flops=FINAL_FLOPS, bytes_accessed=1024, transcendentals=0),
        name=name,
    )(*inputs)


def shards(volume, plane_weight, norm_gain, expand_weight, down_weight, depth_weight):
    depth, extent, count, channels = volume.shape
    wide = expand_weight.shape[2]
    reaches = (FIRST_DILATION // depth, SECOND_DILATION // depth)
    volume, plane_weight, norm_gain, expand_weight, down_weight = map(
        in_hbm, (volume, plane_weight, norm_gain, expand_weight, down_weight)
    )

    def array(*shape):
        return jax.ShapeDtypeStruct(shape, BF16)

    def plane(rows):
        return array(rows, count, channels)

    dense_shape = array(channels // LANES, 5, 6 * LANES, 2 * LANES)
    up_shape, down_shape = array(*expand_weight.shape[1:]), array(*down_weight.shape[1:])
    lead, rest = LEAD, extent - LEAD
    front, back = lead + MARGIN, rest - MARGIN

    def scratch(chunks, copies=0):
        return mix_scratch(chunks, count, channels, wide) + [pltpu.SemaphoreType.DMA((copies,))] * (copies > 0)

    chunks = split(front // 2)
    mixed_a, rows, taps, up, down, gain, dense = call(
        functools.partial(first_a_kernel, chunks), "first_a",
        [plane(front), plane(extent), array(*plane_weight.shape), up_shape, down_shape, array(*norm_gain.shape), dense_shape],
        (volume, plane_weight, expand_weight, down_weight, norm_gain), [HBM] * 5, scratch(chunks, 7), front // 2,
    )
    got_a = exchanged(mixed_a, reaches[0])
    chunks = split(back // 2)
    mixed_b, up_next, down_next, dense_next = call(
        functools.partial(first_b_kernel, chunks), "first_b", [plane(back), up_shape, down_shape, dense_shape],
        (rows, taps, up, down, gain, dense, expand_weight, down_weight), [VMEM] * 6 + [HBM] * 2,
        scratch(chunks, 2), back // 2,
    )
    got_b = exchanged(mixed_b, reaches[0])
    shared = (up_next, down_next, gain, dense_next, depth_weight)
    chunks = split(lead // 2)
    current_a, wide_a = call(
        functools.partial(second_a_kernel, chunks, reaches[0]), "second_a", [plane(front), plane(lead)],
        (rows, mixed_a, *got_a[::-1], *shared), [VMEM] * 9, scratch(chunks), lead // 2,
    )
    far_a = exchanged(wide_a, reaches[1])
    chunks = split(rest // 2)
    current_b, wide_b = call(
        functools.partial(second_b_kernel, chunks, reaches[0]), "second_b", [plane(back), plane(rest)],
        (rows, current_a, mixed_b, *got_b[::-1], *shared), [VMEM] * 10, scratch(chunks), rest // 2,
    )
    far_b = exchanged(wide_b, reaches[1])
    features = final(
        functools.partial(final_a_kernel, reaches[1]), "final_a", volume.shape, lead, {},
        depth_weight, current_a, wide_a, *far_a[::-1],
    )
    return final(
        functools.partial(final_b_kernel, reaches[1]), "final_b", volume.shape, rest, {6: 0},
        depth_weight, current_a, current_b, wide_b, *far_b, features,
    )


def solution(mesh):
    placed = (P(("parts", "slab"), None, None, None), P(), P(), P(), P(), P())
    return jax.shard_map(
        shards,
        mesh=mesh,
        in_specs=placed,
        out_specs=P(("parts", "slab"), None, None, None),
        check_vma=False,
    )
```
